512 devices in a mesh: dp: 4 (over z_hi), ctx: 128 (over x, z_lo, y, core).
Axes of the slice: x: 4, y: 8, z: 8 (z_hi: 4, z_lo: 2; z = z_hi * 2 + z_lo), core: 2. Of those that a mesh axis runs over, the one named last changes fastest.
Arguments:
- values: bfloat16 [4, 16384, 512], P('dp', 'ctx'), may hold values from -6 to 6
- gates: bfloat16 [4, 16384, 512], P('dp', 'ctx'), may hold values from -6 to 6
- grad_out: bfloat16 [4, 16384, 512], P('dp', 'ctx'), may hold values from -6 to 6
- filters: float32 [512, 16384], P('ctx'), may hold values from -6 to 6
- skip: float32 [512], P('ctx'), may hold values from 0.5 to 1.5
Outputs:
- grad_values: bfloat16 [4, 16384, 512], P('dp', 'ctx')
- grad_gates: bfloat16 [4, 16384, 512], P('dp', 'ctx')
- grad_filters: float32 [512, 16384], P('ctx')
The draws below stay inside these ranges and needn't reach their ends.
All inputs are finite; a program needn't handle non-finite values.
Results may differ from the reference program's by a relative error of at most 0.0049.
Values may be sent and summed in bfloat16 or wider, within the bound.
A program may use at most 64 MiB of HBM per device.

```python
import jax
import jax.numpy as jnp
from jax import lax

CH = 512
LENGTH = 16384
SEQS = 4


def block_levels(stream_key, extent, cuts, least, largest):
    level = 1.0
    for axis_at, shards_of in cuts:
        heights = jax.random.uniform(jax.random.fold_in(jax.random.fold_in(stream_key, 6), axis_at), (shards_of,), jnp.float32, least / len(cuts), largest / len(cuts))
        level = level * jnp.repeat(jnp.exp(heights), extent[axis_at] // shards_of).reshape((-1,) + (1,) * (len(extent) - 1 - axis_at))
    return level


def bell_draw(own_key, extent, spread, most, pieces=(), dtype=jnp.bfloat16):
    factor_of = block_levels(own_key, extent, pieces, -0.22, 0.18) if pieces else 1.0
    drawn = jax.random.normal(own_key, extent, jnp.float32) * spread * factor_of
    return jnp.minimum(jnp.maximum(drawn, -most), most).astype(dtype)


def setup_inputs(seed: int = 0) -> dict:
    splits = jax.random.split(jax.random.key(seed), 6)
    values = bell_draw(splits[0], (SEQS, LENGTH, CH), 1.0, 6.0, ((0, 4), (1, 128)))
    gates = bell_draw(splits[1], (SEQS, LENGTH, CH), 1.0, 6.0, ((0, 4), (1, 128)))
    grad_out = bell_draw(splits[2], (SEQS, LENGTH, CH), 1.0, 6.0, ((0, 4), (1, 128)))
    filters = bell_draw(splits[3], (CH, LENGTH), 1.0, 6.0, ((0, 128),), jnp.float32)
    skip = jnp.clip(0.5 + 1.0 * jax.random.uniform(splits[4], (CH,), jnp.float32) ** block_levels(splits[4], (CH,), ((0, 128),), -0.2, 0.2), 0.5, 1.5)
    return {"values": values, "gates": gates, "grad_out": grad_out, "filters": filters, "skip": skip}


def reference(values, gates, grad_out, filters, skip):
    length = values.shape[1]
    count = 2 * length
    scale_a = length ** -0.5
    scale_b = (values.shape[0] * length) ** -0.5
    filt_spec = jnp.fft.rfft(filters, n=count, axis=1)
    gains = skip[:, None]

    def one_seq(total, inputs):
        vals, gate, grad = inputs
        grad_f = grad.astype(jnp.float32)
        grad_conv = (grad_f * gate.astype(jnp.float32)).astype(jnp.bfloat16)
        grad_conv = lax.optimization_barrier(grad_conv)
        vals_t = vals.astype(jnp.float32).T
        dz_t = grad_conv.astype(jnp.float32).T
        vals_spec = jnp.fft.rfft(vals_t, n=count, axis=1)
        dz_spec = jnp.fft.rfft(dz_t, n=count, axis=1)
        conv_raw = jnp.fft.irfft(filt_spec * vals_spec, n=count, axis=1)[:, :length]
        conv = (scale_a * conv_raw + gains * vals_t).astype(jnp.bfloat16)
        conv = lax.optimization_barrier(conv)
        grad_gate = (grad_f * conv.astype(jnp.float32).T).astype(jnp.bfloat16)
        corr = jnp.fft.irfft(jnp.conj(filt_spec) * dz_spec, n=count, axis=1)[:, :length]
        grad_val = (scale_a * corr + gains * dz_t).T.astype(jnp.bfloat16)
        cross = jnp.fft.irfft(jnp.conj(vals_spec) * dz_spec, n=count, axis=1)[:, :length]
        return total + cross, (grad_val, grad_gate)

    start = jnp.zeros(filters.shape, jnp.float32)
    total, (grad_values, grad_gates) = lax.scan(one_seq, start, (values, gates, grad_out))
    return grad_values, grad_gates, scale_b * total
```

```python
import functools

import jax
import jax.numpy as jnp
import numpy as np
from jax import lax
from jax.experimental import pallas as pl
from jax.experimental.pallas import tpu as pltpu
from jax.sharding import PartitionSpec as P

MESH = pl.DeviceIdType.MESH
F32 = jnp.float32
BF16 = jnp.bfloat16


def split_table(table):
    table = np.asarray(table, np.float32)
    high = table.astype(jnp.bfloat16)
    low = (table - high.astype(np.float32)).astype(jnp.bfloat16)
    return high, low


def make_tables(n):
    line = np.arange(n, dtype=np.float64)
    turn = 2.0 * np.pi
    angle_one = turn * np.outer(line + 0.25, line) / n
    angle_mid = turn * np.outer(line + 0.25, line) / (n * n)
    angle_two = turn * (np.outer(line, line) % n) / n
    cos_one, sin_one = np.cos(angle_one), np.sin(angle_one)
    cos_two, sin_two = np.cos(angle_two), np.sin(angle_two)
    first_hi, first_lo = split_table(np.concatenate([cos_one, -sin_one], 0))
    first = np.concatenate([first_hi, first_lo], 1)
    fwd_hi, fwd_lo = split_table(np.block([[cos_two, -sin_two], [sin_two, cos_two]]))
    inv_hi, inv_lo = split_table(np.block([[cos_two, sin_two], [-sin_two, cos_two]]))
    last_hi, last_lo = split_table(np.concatenate([cos_one.T, -sin_one.T], 1))
    last = np.concatenate([last_hi, last_lo], 0)
    pick = np.zeros((256, 256), np.float32)
    for dest in range(32):
        for row in range(4):
            pick[8 * dest + row, 4 * dest + row] = 1.0
            pick[8 * dest + 4 + row, 128 + 4 * dest + row] = 1.0
    wide = np.stack([first, fwd_hi, fwd_lo, inv_hi, inv_lo, last, pick.astype(jnp.bfloat16)])
    eye = np.eye(n, dtype=np.float32).astype(jnp.bfloat16)
    mid = np.stack([np.cos(angle_mid), np.sin(angle_mid)]).astype(np.float32)
    return wide, eye, mid


def mm(a, b):
    return jnp.dot(a, b, preferred_element_type=F32)


def mm_t(a, b):
    return lax.dot_general(a, b, (((1,), (1,)), ((), ())), preferred_element_type=F32)


def split(x):
    high = x.astype(BF16)
    return high, (x - high.astype(F32)).astype(BF16)


def kernel(
    dims,
    vals_ref,
    gate_ref,
    grad_ref,
    filt_ref,
    skip_ref,
    wide_ref,
    eye_ref,
    mid_ref,
    gval_ref,
    ggate_ref,
    gfilt_ref,
    out_box,
    in_box,
    back_box,
    home_box,
    rows,
    hspec,
    spec,
    cross,
    parts,
    whole,
    sems,
):
    n, seqs, nx, nz, ny, nc = dims
    ctx = n
    chans = 4
    me = lax.axis_index("ctx")
    my_seq = lax.axis_index("dp")
    my_c = me % nc
    my_y = (me // nc) % ny
    my_z = (me // (nc * ny)) % nz
    my_x = me // (nc * ny * nz)

    def peer_of(step):
        c = (my_c + step % nc) % nc
        x = (my_x + (step // nc) % nx) % nx
        z = (my_z + (step // (nc * nx)) % nz) % nz
        y = (my_y + step // (nc * nx * nz)) % ny
        return ((x * nz + z) * ny + y) * nc + c

    barrier = pltpu.get_barrier_semaphore()

    def greet(step, carry):
        pl.semaphore_signal(
            barrier, inc=1, device_id=(my_seq, peer_of(step)), device_id_type=MESH
        )
        return carry

    lax.fori_loop(1, ctx, greet, 0)
    for other in range(1, seqs):
        pl.semaphore_signal(
            barrier, inc=1, device_id=((my_seq + other) % seqs, me), device_id_type=MESH
        )

    first, fwd_hi, fwd_lo = wide_ref[0], wide_ref[1], wide_ref[2]
    inv_hi, inv_lo, last, pick = wide_ref[3], wide_ref[4], wide_ref[5], wide_ref[6]
    cos_mid, sin_mid = mid_ref[0], mid_ref[1]

    for g in range(chans):
        cols = slice(128 * g, 128 * (g + 1))
        gated = (grad_ref[:, cols].astype(F32) * gate_ref[:, cols].astype(F32)).astype(BF16)
        both = jnp.concatenate([vals_ref[:, cols], gated], 1)
        out_box[32 * g : 32 * (g + 1)] = mm_t(pick, both).astype(BF16).reshape(32, 8, n)

    pl.semaphore_wait(barrier, ctx - 1 + seqs - 1)

    def exchange(src, dst, send_sem, recv_sem):
        def send(step, carry):
            peer = peer_of(step)
            pltpu.make_async_remote_copy(
                src_ref=src.at[peer],
                dst_ref=dst.at[me],
                send_sem=send_sem,
                recv_sem=recv_sem,
                device_id=(my_seq, peer),
                device_id_type=MESH,
            ).start()
            return carry

        lax.fori_loop(1, ctx, send, 0)
        pltpu.make_async_copy(src.at[me], dst.at[me], recv_sem).start()

    def drain(box, sem, count):
        part = box.at[pl.ds(0, count)]
        pltpu.make_async_copy(part, part, sem).wait()

    exchange(out_box, in_box, sems.at[0], sems.at[1])

    def forward(blocks, exact):
        count = len(blocks)
        data = jnp.concatenate(blocks, 1)
        if exact:
            data = data.astype(BF16)
            part = mm(first, jnp.concatenate([data, data], 0))
        else:
            high, low = split(data)
            part = mm(first, jnp.concatenate([high, high], 0)) + mm(first[:, :n], low)
        turned = []
        for i in range(count):
            re = part[:n, n * i : n * (i + 1)]
            im = part[n:, n * i : n * (i + 1)]
            turned.append(
                jnp.concatenate([re * cos_mid + im * sin_mid, im * cos_mid - re * sin_mid], 1)
            )
        high, low = split(jnp.concatenate(turned, 0))
        return mm(high, fwd_hi) + (mm(low, fwd_hi) + mm(high, fwd_lo))

    def inverse(re, im):
        high, low = split(jnp.concatenate([re, im], 1))
        part = mm(high, inv_hi) + (mm(low, inv_hi) + mm(high, inv_lo))
        res, ims = [], []
        for i in range(chans):
            re = part[n * i : n * (i + 1), :n]
            im = part[n * i : n * (i + 1), n:]
            res.append(re * cos_mid - im * sin_mid)
            ims.append(im * cos_mid + re * sin_mid)
        high, low = split(
            jnp.concatenate([jnp.concatenate(res, 1), jnp.concatenate(ims, 1)], 0)
        )
        both = mm(last, high)
        return both[:n] + (both[n:] + mm(last[:n], low))

    scale = float(n) ** -1
    unit = float(n) ** -2
    h = forward([filt_ref[pl.ds(c, n, stride=chans), :] for c in range(chans)], False)
    for c in range(chans):
        band = slice(n * c, n * (c + 1))
        hspec[band, :n] = (h[band, :n] * scale + skip_ref[c]) * unit
        hspec[band, n:] = h[band, n:] * (scale * unit)

    drain(in_box, sems.at[1], ctx)
    rows[...] = in_box[...].astype(F32).reshape(8 * n, n)
    spec[...] = forward([rows[pl.ds(c, n, stride=8), :] for c in range(8)], True)

    half = chans * n
    v_re, v_im = spec[:half, :n], spec[:half, n:]
    d_re, d_im = spec[half:, :n], spec[half:, n:]
    h_re, h_im = hspec[:, :n], hspec[:, n:]

    lag = inverse(d_re * v_re + d_im * v_im, d_im * v_re - d_re * v_im)
    lag = lag * (unit * (seqs**-0.5) * scale)
    for c in range(chans):
        cross[c] = lag[:, n * c : n * (c + 1)]
    for other in range(1, seqs):
        peer = (my_seq + other) % seqs
        pltpu.make_async_remote_copy(
            src_ref=cross.at[peer],
            dst_ref=parts.at[my_seq],
            send_sem=sems.at[4],
            recv_sem=sems.at[5],
            device_id=(peer, me),
            device_id_type=MESH,
        ).start()
    pltpu.make_async_copy(cross.at[my_seq], parts.at[my_seq], sems.at[5]).start()

    conv = inverse(h_re * v_re - h_im * v_im, h_re * v_im + h_im * v_re)
    gval = inverse(h_re * d_re + h_im * d_im, h_re * d_im - h_im * d_re)
    for c in range(chans):
        rows[pl.ds(c, n, stride=8), :] = conv[:, n * c : n * (c + 1)]
        rows[pl.ds(chans + c, n, stride=8), :] = gval[:, n * c : n * (c + 1)]
    back_box[...] = rows[...].reshape(n, 8, n).astype(BF16)
    exchange(back_box, home_box, sems.at[2], sems.at[3])

    drain(parts, sems.at[5], seqs)
    total = (parts[0] + parts[1]) + (parts[2] + parts[3])
    cross_sent = cross.at[pl.ds(0, seqs - 1)]
    pltpu.make_async_copy(cross_sent, cross_sent, sems.at[4]).wait()
    cross[0] = total
    for other in range(1, seqs):
        peer = (my_seq + other) % seqs
        pltpu.make_async_remote_copy(
            src_ref=cross.at[0],
            dst_ref=whole.at[my_seq],
            send_sem=sems.at[6],
            recv_sem=sems.at[7],
            device_id=(peer, me),
            device_id_type=MESH,
        ).start()
    pltpu.make_async_copy(cross.at[0], whole.at[my_seq], sems.at[7]).start()
    drain(whole, sems.at[7], seqs)
    for c in range(chans):
        gfilt_ref[pl.ds(c, n, stride=chans), :] = whole[c]

    drain(home_box, sems.at[3], ctx)
    for g in range(chans):
        cols = slice(128 * g, 128 * (g + 1))
        group = home_box[32 * g : 32 * (g + 1)].reshape(256, n)
        both = mm(mm_t(eye_ref[...], group).astype(BF16), pick)
        gval_ref[:, cols] = both[:, n:].astype(BF16)
        ggate_ref[:, cols] = (grad_ref[:, cols].astype(F32) * both[:, :n]).astype(BF16)

    drain(out_box, sems.at[0], ctx - 1)
    drain(back_box, sems.at[2], ctx - 1)
    drain(cross, sems.at[6], seqs - 1)


def per_device(sizes, values, gates, grad_out, filters, skip):
    seqs, ctx = sizes
    length = filters.shape[1]
    n = values.shape[1]
    chans = filters.shape[0]
    wide, eye, mid = (jnp.asarray(t) for t in make_tables(n))
    filt = filters.reshape(chans, n, n).transpose(1, 0, 2).reshape(n * chans, n)
    vmem = pl.BlockSpec(memory_space=pltpu.VMEM)
    smem = pl.BlockSpec(memory_space=pltpu.SMEM)
    gval, ggate, gfilt = pl.pallas_call(
        functools.partial(kernel, (n, seqs, 4, 2, 8, 2)),
        name="hyena_bwd",
        out_shape=(
            jax.ShapeDtypeStruct(values.shape[1:], BF16),
            jax.ShapeDtypeStruct(values.shape[1:], BF16),
            jax.ShapeDtypeStruct((n * chans, n), F32),
        ),
        in_specs=[vmem] * 4 + [smem] + [vmem] * 3,
        out_specs=(vmem,) * 3,
        scratch_shapes=[
            pltpu.VMEM((n, 8, n), BF16),
            pltpu.VMEM((n, 8, n), BF16),
            pltpu.VMEM((n, 8, n), BF16),
            pltpu.VMEM((n, 8, n), BF16),
            pltpu.VMEM((8 * n, n), F32),
            pltpu.VMEM((chans * n, 2 * n), F32),
            pltpu.VMEM((2 * chans * n, 2 * n), F32),
            pltpu.VMEM((chans, n, n), F32),
            pltpu.VMEM((seqs, n, n), F32),
            pltpu.VMEM((seqs, n, n), F32),
            pltpu.SemaphoreType.DMA((8,)),
        ],
        compiler_params=pltpu.CompilerParams(collective_id=0, has_side_effects=True),
    )(values[0], gates[0], grad_out[0], filt, skip, wide, eye, mid)
    gfilt = gfilt.reshape(n, chans, n).transpose(1, 0, 2).reshape(chans, length)
    return gval[None], ggate[None], gfilt


def solution(mesh):
    in_specs = (
        P("dp", "ctx", None),
        P("dp", "ctx", None),
        P("dp", "ctx", None),
        P("ctx", None),
        P("ctx"),
    )
    out_specs = (P("dp", "ctx", None), P("dp", "ctx", None), P("ctx", None))
    return jax.shard_map(
        functools.partial(per_device, (mesh.shape["dp"], mesh.shape["ctx"])),
        mesh=mesh,
        in_specs=in_specs,
        out_specs=out_specs,
        check_vma=False,
    )
```

```python
import functools

import jax
import jax.numpy as jnp
import numpy as np
from jax import lax
from jax.experimental import pallas as pl
from jax.experimental.pallas import tpu as pltpu
from jax.sharding import PartitionSpec as P

MESH = pl.DeviceIdType.MESH
F32 = jnp.float32
BF16 = jnp.bfloat16


def split_table(table):
    table = np.asarray(table, np.float32)
    high = table.astype(jnp.bfloat16)
    low = (table - high.astype(np.float32)).astype(jnp.bfloat16)
    return high, low


def make_tables(n):
    line = np.arange(n, dtype=np.float64)
    turn = 2.0 * np.pi
    angle_one = turn * np.outer(line + 0.25, line) / n
    angle_mid = turn * np.outer(line + 0.25, line) / (n * n)
    angle_two = turn * (np.outer(line, line) % n) / n
    cos_one, sin_one = np.cos(angle_one), np.sin(angle_one)
    cos_two, sin_two = np.cos(angle_two), np.sin(angle_two)
    first_hi, first_lo = split_table(np.concatenate([cos_one, -sin_one], 0))
    first = np.concatenate([first_hi, first_lo], 1)
    fwd_hi, fwd_lo = split_table(np.block([[cos_two, -sin_two], [sin_two, cos_two]]))
    inv_hi, inv_lo = split_table(np.block([[cos_two, sin_two], [-sin_two, cos_two]]))
    last_hi, last_lo = split_table(np.concatenate([cos_one.T, -sin_one.T], 1))
    last = np.concatenate([last_hi, last_lo], 0)
    pick = np.zeros((256, 256), np.float32)
    for dest in range(32):
        for row in range(4):
            pick[8 * dest + row, 4 * dest + row] = 1.0
            pick[8 * dest + 4 + row, 128 + 4 * dest + row] = 1.0
    wide = np.stack([first, fwd_hi, fwd_lo, inv_hi, inv_lo, last, pick.astype(jnp.bfloat16)])
    eye = np.eye(n, dtype=np.float32).astype(jnp.bfloat16)
    mid = np.stack([np.cos(angle_mid), np.sin(angle_mid)]).astype(np.float32)
    return wide, eye, mid


def mm(a, b):
    return jnp.dot(a, b, preferred_element_type=F32)


def mm_t(a, b):
    return lax.dot_general(a, b, (((1,), (1,)), ((), ())), preferred_element_type=F32)


def split(x):
    high = x.astype(BF16)
    return high, (x - high.astype(F32)).astype(BF16)


def kernel(
    dims,
    vals_hbm,
    gate_hbm,
    grad_hbm,
    filt_hbm,
    skip_hbm,
    wide_hbm,
    mid_hbm,
    home_ref,
    whole_ref,
    vals_ref,
    gate_ref,
    grad_ref,
    filt_ref,
    skip_ref,
    wide_ref,
    mid_ref,
    out_box,
    in_box,
    back_box,
    rows,
    hspec,
    spec,
    own,
    cross,
    parts,
    total,
    load_sems,
    sems,
):
    n, seqs, nx, nz, ny, nc = dims
    ctx = n
    chans = 4
    me = lax.axis_index("ctx")
    my_seq = lax.axis_index("dp")

    loads = []
    for i, (src, dst) in enumerate(
        (
            (grad_hbm, grad_ref),
            (gate_hbm, gate_ref),
            (vals_hbm, vals_ref),
            (wide_hbm, wide_ref),
            (filt_hbm, filt_ref),
            (mid_hbm, mid_ref),
            (skip_hbm, skip_ref),
        )
    ):
        loads.append(pltpu.make_async_copy(src, dst, load_sems.at[i]))
        loads[-1].start()

    my_c = lax.rem(me, nc)
    my_y = lax.rem(me // nc, ny)
    my_z = lax.rem(me // (nc * ny), nz)
    my_x = me // (nc * ny * nz)
    x_part = [lax.rem(my_x + d, nx) * (nz * ny * nc) for d in range(nx)]
    z_part = [lax.rem(my_z + d, nz) * (ny * nc) for d in range(nz)]
    c_part = [lax.rem(my_c + d, nc) for d in range(nc)]
    lines = [x + z + c for x in x_part for z in z_part for c in c_part]

    def each_peer(visit):
        def plane(step, carry):
            y = lax.rem(my_y + step, ny) * nc
            for line in lines:
                visit(line + y)
            return carry

        lax.fori_loop(ny // 2, ny, plane, 0)
        lax.fori_loop(1, ny // 2, plane, 0)
        for line in lines[1:]:
            visit(line + my_y * nc)

    barrier = pltpu.get_barrier_semaphore()

    def greet(peer):
        pl.semaphore_signal(
            barrier, inc=1, device_id=(my_seq, peer), device_id_type=MESH
        )

    each_peer(greet)
    others = [lax.rem(my_seq + d, seqs) for d in range(seqs)]
    for d in range(1, seqs):
        pl.semaphore_signal(
            barrier, inc=1, device_id=(others[d], me), device_id_type=MESH
        )

    for load in loads[:4]:
        load.wait()
    first, fwd_hi, fwd_lo = wide_ref[0], wide_ref[1], wide_ref[2]
    inv_hi, inv_lo, last, pick = wide_ref[3], wide_ref[4], wide_ref[5], wide_ref[6]

    for g in range(chans):
        cols = slice(128 * g, 128 * (g + 1))
        gated = (grad_ref[:, cols].astype(F32) * gate_ref[:, cols].astype(F32)).astype(BF16)
        both = jnp.concatenate([vals_ref[:, cols], gated], 1)
        out_box[32 * g : 32 * (g + 1)] = mm_t(pick, both).astype(BF16).reshape(32, 8, n)

    pl.semaphore_wait(barrier, ctx - 1 + seqs - 1)

    def exchange(src, dst, send_sem, recv_sem):
        def send(peer):
            pltpu.make_async_remote_copy(
                src_ref=src.at[peer],
                dst_ref=dst.at[me],
                send_sem=send_sem,
                recv_sem=recv_sem,
                device_id=(my_seq, peer),
                device_id_type=MESH,
            ).start()

        each_peer(send)
        pltpu.make_async_copy(src.at[me], dst.at[me], recv_sem).start()

    def drain(box, sem, count):
        part = box.at[pl.ds(0, count)]
        pltpu.make_async_copy(part, part, sem).wait()

    exchange(out_box, in_box, sems.at[0], sems.at[1])

    for load in loads[4:]:
        load.wait()
    cos_mid, sin_mid = mid_ref[0], mid_ref[1]

    def forward(blocks, exact):
        count = len(blocks)
        data = jnp.concatenate(blocks, 1)
        if exact:
            data = data.astype(BF16)
            part = mm(first, jnp.concatenate([data, data], 0))
        else:
            high, low = split(data)
            part = mm(first, jnp.concatenate([high, high], 0)) + mm(first[:, :n], low)
        turned = []
        for i in range(count):
            re = part[:n, n * i : n * (i + 1)]
            im = part[n:, n * i : n * (i + 1)]
            turned.append(
                jnp.concatenate([re * cos_mid + im * sin_mid, im * cos_mid - re * sin_mid], 1)
            )
        high, low = split(jnp.concatenate(turned, 0))
        return mm(high, fwd_hi) + (mm(low, fwd_hi) + mm(high, fwd_lo))

    def inverse(re, im):
        high, low = split(jnp.concatenate([re, im], 1))
        part = mm(high, inv_hi) + (mm(low, inv_hi) + mm(high, inv_lo))
        res, ims = [], []
        for i in range(chans):
            re = part[n * i : n * (i + 1), :n]
            im = part[n * i : n * (i + 1), n:]
            res.append(re * cos_mid - im * sin_mid)
            ims.append(im * cos_mid + re * sin_mid)
        high, low = split(
            jnp.concatenate([jnp.concatenate(res, 1), jnp.concatenate(ims, 1)], 0)
        )
        both = mm(last, high)
        return both[:n] + (both[n:] + mm(last[:n], low))

    scale = float(n) ** -1
    unit = float(n) ** -2
    h = forward([filt_ref[pl.ds(c, n, stride=chans), :] for c in range(chans)], False)
    for c in range(chans):
        band = slice(n * c, n * (c + 1))
        hspec[band, :n] = (h[band, :n] * scale + skip_ref[c]) * unit
        hspec[band, n:] = h[band, n:] * (scale * unit)

    drain(in_box, sems.at[1], ctx)
    rows[...] = in_box[...].astype(F32).reshape(8 * n, n)
    spec[...] = forward([rows[pl.ds(c, n, stride=8), :] for c in range(8)], True)

    half = chans * n
    v_re, v_im = spec[:half, :n], spec[:half, n:]
    d_re, d_im = spec[half:, :n], spec[half:, n:]
    h_re, h_im = hspec[:, :n], hspec[:, n:]

    lag = inverse(d_re * v_re + d_im * v_im, d_im * v_re - d_re * v_im)
    lag = lag * (unit * (seqs**-0.5) * scale)
    for c in range(chans):
        own[c] = lag[:, n * c : n * (c + 1)]
        cross[c] = lag[:, n * c : n * (c + 1)].astype(BF16)
    far_first = sorted(range(1, seqs), key=lambda d: -min(d, seqs - d))
    for d in far_first:
        pltpu.make_async_remote_copy(
            src_ref=cross.at[others[d]],
            dst_ref=parts.at[d - 1],
            send_sem=sems.at[4],
            recv_sem=sems.at[5],
            device_id=(others[d], me),
            device_id_type=MESH,
        ).start()

    conv = inverse(h_re * v_re - h_im * v_im, h_re * v_im + h_im * v_re)
    gval = inverse(h_re * d_re + h_im * d_im, h_re * d_im - h_im * d_re)
    for c in range(chans):
        rows[pl.ds(c, n, stride=8), :] = conv[:, n * c : n * (c + 1)]
        rows[pl.ds(chans + c, n, stride=8), :] = gval[:, n * c : n * (c + 1)]
    back_box[...] = rows[...].reshape(n, 8, n).astype(BF16)

    @pl.when(my_seq < seqs // 2)
    def _():
        exchange(back_box, home_ref, sems.at[2], sems.at[3])

    drain(parts, sems.at[5], seqs - 1)
    summed = own[my_seq]
    for d in range(seqs - 1):
        summed = summed + parts[d].astype(F32)
    total[0] = summed.astype(BF16)
    for d in far_first:
        pltpu.make_async_remote_copy(
            src_ref=total.at[0],
            dst_ref=whole_ref.at[my_seq],
            send_sem=sems.at[6],
            recv_sem=sems.at[7],
            device_id=(others[d], me),
            device_id_type=MESH,
        ).start()
    pltpu.make_async_copy(total.at[0], whole_ref.at[my_seq], sems.at[7]).start()

    @pl.when(my_seq >= seqs // 2)
    def _():
        exchange(back_box, home_ref, sems.at[2], sems.at[3])

    drain(out_box, sems.at[0], ctx - 1)
    drain(cross, sems.at[4], seqs - 1)
    drain(back_box, sems.at[2], ctx - 1)
    drain(cross, sems.at[6], seqs - 1)
    drain(home_ref, sems.at[3], ctx)
    drain(whole_ref, sems.at[7], seqs)


def finish(home_ref, whole_ref, grad_ref, pick_ref, eye_ref, gval_ref, ggate_ref, gfilt_ref):
    n = grad_ref.shape[0]
    chans = whole_ref.shape[0]
    pick = pick_ref[...]
    for c in range(chans):
        gfilt_ref[pl.ds(c, n, stride=chans), :] = whole_ref[c].astype(F32)
    for g in range(chans):
        cols = slice(128 * g, 128 * (g + 1))
        group = home_ref[32 * g : 32 * (g + 1)].reshape(256, n)
        both = mm(mm_t(eye_ref[...], group).astype(BF16), pick)
        gval_ref[:, cols] = both[:, n:].astype(BF16)
        ggate_ref[:, cols] = (grad_ref[:, cols].astype(F32) * both[:, :n]).astype(BF16)


def per_device(sizes, values, gates, grad_out, filters, skip):
    seqs, ctx = sizes
    length = filters.shape[1]
    n = values.shape[1]
    chans = filters.shape[0]
    wide, eye, mid = (jnp.asarray(t) for t in make_tables(n))
    pick = jnp.asarray(make_tables(n)[0][6])
    filt = filters.reshape(chans, n, n).transpose(1, 0, 2).reshape(n * chans, n)
    vmem = pl.BlockSpec(memory_space=pltpu.VMEM)
    anywhere = pl.BlockSpec(memory_space=pl.ANY)
    home, whole = pl.pallas_call(
        functools.partial(kernel, (n, seqs, 4, 2, 8, 2)),
        name="hyena_bwd",
        out_shape=(
            jax.ShapeDtypeStruct((n, 8, n), BF16),
            jax.ShapeDtypeStruct((seqs, n, n), BF16),
        ),
        in_specs=[anywhere] * 7,
        out_specs=(anywhere,) * 2,
        scratch_shapes=[
            pltpu.VMEM((n, chans * n), BF16),
            pltpu.VMEM((n, chans * n), BF16),
            pltpu.VMEM((n, chans * n), BF16),
            pltpu.VMEM((n * chans, n), F32),
            pltpu.SMEM((chans,), F32),
            pltpu.VMEM(wide.shape, BF16),
            pltpu.VMEM(mid.shape, F32),
            pltpu.VMEM((n, 8, n), BF16),
            pltpu.VMEM((n, 8, n), BF16),
            pltpu.VMEM((n, 8, n), BF16),
            pltpu.VMEM((8 * n, n), F32),
            pltpu.VMEM((chans * n, 2 * n), F32),
            pltpu.VMEM((2 * chans * n, 2 * n), F32),
            pltpu.VMEM((chans, n, n), F32),
            pltpu.VMEM((chans, n, n), BF16),
            pltpu.VMEM((seqs - 1, n, n), BF16),
            pltpu.VMEM((1, n, n), BF16),
            pltpu.SemaphoreType.DMA((7,)),
            pltpu.SemaphoreType.DMA((8,)),
        ],
        compiler_params=pltpu.CompilerParams(collective_id=0, has_side_effects=True),
    )(values[0], gates[0], grad_out[0], filt, skip, wide, mid)
    gval, ggate, gfilt = pl.pallas_call(
        finish,
        name="hyena_out",
        out_shape=(
            jax.ShapeDtypeStruct(values.shape[1:], BF16),
            jax.ShapeDtypeStruct(values.shape[1:], BF16),
            jax.ShapeDtypeStruct((n * chans, n), F32),
        ),
        in_specs=[vmem] * 5,
        out_specs=(vmem,) * 3,
    )(home, whole, grad_out[0], pick, eye)
    gfilt = gfilt.reshape(n, chans, n).transpose(1, 0, 2).reshape(chans, length)
    return gval[None], ggate[None], gfilt


def solution(mesh):
    in_specs = (
        P("dp", "ctx", None),
        P("dp", "ctx", None),
        P("dp", "ctx", None),
        P("ctx", None),
        P("ctx"),
    )
    out_specs = (P("dp", "ctx", None), P("dp", "ctx", None), P("ctx", None))
    return jax.shard_map(
        functools.partial(per_device, (mesh.shape["dp"], mesh.shape["ctx"])),
        mesh=mesh,
        in_specs=in_specs,
        out_specs=out_specs,
        check_vma=False,
    )
```

```python
import functools

import jax
import jax.numpy as jnp
import numpy as np
from jax import lax
from jax.experimental import pallas as pl
from jax.experimental.pallas import tpu as pltpu
from jax.sharding import PartitionSpec as P

MESH = pl.DeviceIdType.MESH
F32 = jnp.float32
BF16 = jnp.bfloat16


def split_table(table):
    table = np.asarray(table, np.float32)
    high = table.astype(jnp.bfloat16)
    low = (table - high.astype(np.float32)).astype(jnp.bfloat16)
    return high, low


def make_tables(n):
    line = np.arange(n, dtype=np.float64)
    turn = 2.0 * np.pi
    angle_one = turn * np.outer(line + 0.25, line) / n
    angle_mid = turn * np.outer(line + 0.25, line) / (n * n)
    angle_two = turn * (np.outer(line, line) % n) / n
    cos_one, sin_one = np.cos(angle_one), np.sin(angle_one)
    cos_two, sin_two = np.cos(angle_two), np.sin(angle_two)
    first_hi, first_lo = split_table(np.concatenate([cos_one, -sin_one], 0))
    first = np.concatenate([first_hi, first_lo], 1)
    fwd_hi, fwd_lo = split_table(np.block([[cos_two, -sin_two], [sin_two, cos_two]]))
    inv_hi, inv_lo = split_table(np.block([[cos_two, sin_two], [-sin_two, cos_two]]))
    last_hi, last_lo = split_table(np.concatenate([cos_one.T, -sin_one.T], 1))
    last = np.concatenate([last_hi, last_lo], 0)
    pick = np.zeros((256, 256), np.float32)
    for dest in range(32):
        for row in range(4):
            pick[8 * dest + row, 4 * dest + row] = 1.0
            pick[8 * dest + 4 + row, 128 + 4 * dest + row] = 1.0
    wide = np.stack([first, fwd_hi, fwd_lo, inv_hi, inv_lo, last, pick.astype(jnp.bfloat16)])
    eye = np.eye(n, dtype=np.float32).astype(jnp.bfloat16)
    mid = np.stack([np.cos(angle_mid), np.sin(angle_mid)]).astype(np.float32)
    return wide, eye, mid


def mm(a, b):
    return jnp.dot(a, b, preferred_element_type=F32)


def mm_t(a, b):
    return lax.dot_general(a, b, (((1,), (1,)), ((), ())), preferred_element_type=F32)


def split(x):
    high = x.astype(BF16)
    return high, (x - high.astype(F32)).astype(BF16)


def kernel(
    dims,
    vals_hbm,
    gate_hbm,
    grad_hbm,
    filt_hbm,
    skip_hbm,
    wide_hbm,
    mid_hbm,
    home_ref,
    whole_ref,
    vals_ref,
    gate_ref,
    grad_ref,
    filt_ref,
    skip_ref,
    wide_ref,
    mid_ref,
    out_box,
    in_box,
    back_box,
    rows,
    hspec,
    spec,
    own,
    cross,
    parts,
    total,
    load_sems,
    sems,
    ready,
):
    n, seqs, nx, nz, ny, nc = dims
    ctx = n
    chans = 4
    me = lax.axis_index("ctx")
    my_seq = lax.axis_index("dp")

    loads = []
    for i, (src, dst) in enumerate(
        (
            (grad_hbm, grad_ref),
            (gate_hbm, gate_ref),
            (vals_hbm, vals_ref),
            (wide_hbm, wide_ref),
            (filt_hbm, filt_ref),
            (mid_hbm, mid_ref),
            (skip_hbm, skip_ref),
        )
    ):
        loads.append(pltpu.make_async_copy(src, dst, load_sems.at[i]))
        loads[-1].start()

    my_c = lax.rem(me, nc)
    my_y = lax.rem(me // nc, ny)
    my_z = lax.rem(me // (nc * ny), nz)
    my_x = me // (nc * ny * nz)
    x_part = [lax.rem(my_x + d, nx) * (nz * ny * nc) for d in range(nx)]
    z_part = [lax.rem(my_z + d, nz) * (ny * nc) for d in range(nz)]
    c_part = [lax.rem(my_c + d, nc) for d in range(nc)]
    lines = [x + z + c for x in x_part for z in z_part for c in c_part]

    def each_peer(visit):
        def plane(step, carry):
            y = lax.rem(my_y + step, ny) * nc
            for line in lines:
                visit(line + y)
            return carry

        lax.fori_loop(ny // 2, ny, plane, 0)
        lax.fori_loop(1, ny // 2, plane, 0)
        for line in lines[1:]:
            visit(line + my_y * nc)

    barrier = pltpu.get_barrier_semaphore()

    def greet(peer):
        pl.semaphore_signal(
            barrier, inc=1, device_id=(my_seq, peer), device_id_type=MESH
        )

    each_peer(greet)
    others = [lax.rem(my_seq + d, seqs) for d in range(seqs)]
    for d in range(1, seqs):

        @pl.when(my_seq + d < seqs)
        def _(d=d):
            pl.semaphore_signal(
                barrier, inc=1, device_id=(others[d], me), device_id_type=MESH
            )

    for load in loads[:4]:
        load.wait()
    first, fwd_hi, fwd_lo = wide_ref[0], wide_ref[1], wide_ref[2]
    inv_hi, inv_lo, last, pick = wide_ref[3], wide_ref[4], wide_ref[5], wide_ref[6]

    for g in range(chans):
        cols = slice(128 * g, 128 * (g + 1))
        gated = (grad_ref[:, cols].astype(F32) * gate_ref[:, cols].astype(F32)).astype(BF16)
        both = jnp.concatenate([vals_ref[:, cols], gated], 1)
        out_box[32 * g : 32 * (g + 1)] = mm_t(pick, both).astype(BF16).reshape(32, 8, n)

    pl.semaphore_wait(barrier, ctx - 1 + my_seq)

    def exchange(src, dst, send_sem, recv_sem):
        def send(peer):
            pltpu.make_async_remote_copy(
                src_ref=src.at[peer],
                dst_ref=dst.at[me],
                send_sem=send_sem,
                recv_sem=recv_sem,
                device_id=(my_seq, peer),
                device_id_type=MESH,
            ).start()

        each_peer(send)
        pltpu.make_async_copy(src.at[me], dst.at[me], recv_sem).start()

    def drain(box, sem, count):
        part = box.at[pl.ds(0, count)]
        pltpu.make_async_copy(part, part, sem).wait()

    exchange(out_box, in_box, sems.at[0], sems.at[1])
    for d in range(1, seqs):

        @pl.when(my_seq + d >= seqs)
        def _(d=d):
            pl.semaphore_signal(
                ready, inc=1, device_id=(others[d], me), device_id_type=MESH
            )

    for load in loads[4:]:
        load.wait()
    cos_mid, sin_mid = mid_ref[0], mid_ref[1]

    def forward(blocks, exact):
        count = len(blocks)
        data = jnp.concatenate(blocks, 1)
        if exact:
            data = data.astype(BF16)
            part = mm(first, jnp.concatenate([data, data], 0))
        else:
            high, low = split(data)
            part = mm(first, jnp.concatenate([high, high], 0)) + mm(first[:, :n], low)
        turned = []
        for i in range(count):
            re = part[:n, n * i : n * (i + 1)]
            im = part[n:, n * i : n * (i + 1)]
            turned.append(
                jnp.concatenate([re * cos_mid + im * sin_mid, im * cos_mid - re * sin_mid], 1)
            )
        high, low = split(jnp.concatenate(turned, 0))
        return mm(high, fwd_hi) + (mm(low, fwd_hi) + mm(high, fwd_lo))

    def inverse(re, im):
        high, low = split(jnp.concatenate([re, im], 1))
        part = mm(high, inv_hi) + (mm(low, inv_hi) + mm(high, inv_lo))
        res, ims = [], []
        for i in range(chans):
            re = part[n * i : n * (i + 1), :n]
            im = part[n * i : n * (i + 1), n:]
            res.append(re * cos_mid - im * sin_mid)
            ims.append(im * cos_mid + re * sin_mid)
        high, low = split(
            jnp.concatenate([jnp.concatenate(res, 1), jnp.concatenate(ims, 1)], 0)
        )
        both = mm(last, high)
        return both[:n] + (both[n:] + mm(last[:n], low))

    scale = float(n) ** -1
    unit = float(n) ** -2
    h = forward([filt_ref[pl.ds(c, n, stride=chans), :] for c in range(chans)], False)
    for c in range(chans):
        band = slice(n * c, n * (c + 1))
        hspec[band, :n] = (h[band, :n] * scale + skip_ref[c]) * unit
        hspec[band, n:] = h[band, n:] * (scale * unit)

    drain(in_box, sems.at[1], ctx)
    rows[...] = in_box[...].astype(F32).reshape(8 * n, n)
    spec[...] = forward([rows[pl.ds(c, n, stride=8), :] for c in range(8)], True)

    half = chans * n

    def send_back():
        v_re, v_im = spec[:half, :n], spec[:half, n:]
        d_re, d_im = spec[half:, :n], spec[half:, n:]
        h_re, h_im = hspec[:, :n], hspec[:, n:]
        conv = inverse(h_re * v_re - h_im * v_im, h_re * v_im + h_im * v_re)
        gval = inverse(h_re * d_re + h_im * d_im, h_re * d_im - h_im * d_re)
        for c in range(chans):
            rows[pl.ds(c, n, stride=8), :] = conv[:, n * c : n * (c + 1)]
            rows[pl.ds(chans + c, n, stride=8), :] = gval[:, n * c : n * (c + 1)]
        back_box[...] = rows[...].reshape(n, 8, n).astype(BF16)
        exchange(back_box, home_ref, sems.at[2], sems.at[3])

    early = my_seq < seqs // 2

    v_re, v_im = spec[:half, :n], spec[:half, n:]
    d_re, d_im = spec[half:, :n], spec[half:, n:]
    lag = inverse(d_re * v_re + d_im * v_im, d_im * v_re - d_re * v_im)
    lag = lag * (unit * (seqs**-0.5) * scale)
    for c in range(chans):
        own[c] = lag[:, n * c : n * (c + 1)]
        cross[c] = lag[:, n * c : n * (c + 1)].astype(BF16)
    far_first = sorted(range(1, seqs), key=lambda d: -min(d, seqs - d))

    @pl.when(my_seq < seqs - 1)
    def _():
        pl.semaphore_wait(ready, seqs - 1 - my_seq)

    for d in far_first:
        pltpu.make_async_remote_copy(
            src_ref=cross.at[others[d]],
            dst_ref=parts.at[d - 1],
            send_sem=sems.at[4],
            recv_sem=sems.at[5],
            device_id=(others[d], me),
            device_id_type=MESH,
        ).start()

    pl.when(early)(send_back)
    drain(parts, sems.at[5], seqs - 1)
    summed = own[my_seq]
    for d in range(seqs - 1):
        summed = summed + parts[d].astype(F32)
    total[0] = summed.astype(BF16)
    for d in far_first:
        pltpu.make_async_remote_copy(
            src_ref=total.at[0],
            dst_ref=whole_ref.at[my_seq],
            send_sem=sems.at[6],
            recv_sem=sems.at[7],
            device_id=(others[d], me),
            device_id_type=MESH,
        ).start()
    pltpu.make_async_copy(total.at[0], whole_ref.at[my_seq], sems.at[7]).start()

    pl.when(jnp.logical_not(early))(send_back)

    drain(out_box, sems.at[0], ctx - 1)
    drain(cross, sems.at[4], seqs - 1)
    drain(back_box, sems.at[2], ctx - 1)
    drain(cross, sems.at[6], seqs - 1)
    drain(home_ref, sems.at[3], ctx)
    drain(whole_ref, sems.at[7], seqs)


def finish(home_ref, whole_ref, grad_ref, pick_ref, eye_ref, gval_ref, ggate_ref, gfilt_ref):
    n = grad_ref.shape[0]
    chans = whole_ref.shape[0]
    pick = pick_ref[...]
    for c in range(chans):
        gfilt_ref[pl.ds(c, n, stride=chans), :] = whole_ref[c].astype(F32)
    for g in range(chans):
        cols = slice(128 * g, 128 * (g + 1))
        group = home_ref[32 * g : 32 * (g + 1)].reshape(256, n)
        both = mm(mm_t(eye_ref[...], group).astype(BF16), pick)
        gval_ref[:, cols] = both[:, n:].astype(BF16)
        ggate_ref[:, cols] = (grad_ref[:, cols].astype(F32) * both[:, :n]).astype(BF16)


def per_device(sizes, values, gates, grad_out, filters, skip):
    seqs, ctx = sizes
    length = filters.shape[1]
    n = values.shape[1]
    chans = filters.shape[0]
    wide, eye, mid = (jnp.asarray(t) for t in make_tables(n))
    pick = jnp.asarray(make_tables(n)[0][6])
    filt = filters.reshape(chans, n, n).transpose(1, 0, 2).reshape(n * chans, n)
    vmem = pl.BlockSpec(memory_space=pltpu.VMEM)
    anywhere = pl.BlockSpec(memory_space=pl.ANY)
    in_hbm = pl.BlockSpec(memory_space=pltpu.HBM)
    home, whole = pl.pallas_call(
        functools.partial(kernel, (n, seqs, 4, 2, 8, 2)),
        name="hyena_bwd",
        out_shape=(
            pltpu.VMEM((n, 8, n), BF16),
            pltpu.VMEM((seqs, n, n), BF16),
        ),
        in_specs=[in_hbm] * 7,
        out_specs=(anywhere,) * 2,
        scratch_shapes=[
            pltpu.VMEM((n, chans * n), BF16),
            pltpu.VMEM((n, chans * n), BF16),
            pltpu.VMEM((n, chans * n), BF16),
            pltpu.VMEM((n * chans, n), F32),
            pltpu.SMEM((chans,), F32),
            pltpu.VMEM(wide.shape, BF16),
            pltpu.VMEM(mid.shape, F32),
            pltpu.VMEM((n, 8, n), BF16),
            pltpu.VMEM((n, 8, n), BF16),
            pltpu.VMEM((n, 8, n), BF16),
            pltpu.VMEM((8 * n, n), F32),
            pltpu.VMEM((chans * n, 2 * n), F32),
            pltpu.VMEM((2 * chans * n, 2 * n), F32),
            pltpu.VMEM((chans, n, n), F32),
            pltpu.VMEM((chans, n, n), BF16),
            pltpu.VMEM((seqs - 1, n, n), BF16),
            pltpu.VMEM((1, n, n), BF16),
            pltpu.SemaphoreType.DMA((7,)),
            pltpu.SemaphoreType.DMA((8,)),
            pltpu.SemaphoreType.REGULAR,
        ],
        compiler_params=pltpu.CompilerParams(
            collective_id=0, has_side_effects=True, vmem_limit_bytes=60 * 1024 * 1024
        ),
    )(values[0], gates[0], grad_out[0], filt, skip, wide, mid)
    gval, ggate, gfilt = pl.pallas_call(
        finish,
        name="hyena_out",
        out_shape=(
            jax.ShapeDtypeStruct(values.shape[1:], BF16),
            jax.ShapeDtypeStruct(values.shape[1:], BF16),
            jax.ShapeDtypeStruct((n * chans, n), F32),
        ),
        in_specs=[vmem] * 5,
        out_specs=(vmem,) * 3,
        compiler_params=pltpu.CompilerParams(vmem_limit_bytes=8 << 20),
    )(home, whole, grad_out[0], pick, eye)
    gfilt = gfilt.reshape(n, chans, n).transpose(1, 0, 2).reshape(chans, length)
    return gval[None], ggate[None], gfilt


def solution(mesh):
    in_specs = (
        P("dp", "ctx", None),
        P("dp", "ctx", None),
        P("dp", "ctx", None),
        P("ctx", None),
        P("ctx"),
    )
    out_specs = (P("dp", "ctx", None), P("dp", "ctx", None), P("ctx", None))
    return jax.shard_map(
        functools.partial(per_device, (mesh.shape["dp"], mesh.shape["ctx"])),
        mesh=mesh,
        in_specs=in_specs,
        out_specs=out_specs,
        check_vma=False,
    )
```

```python
import functools

import jax
import jax.numpy as jnp
import numpy as np
from jax import lax
from jax.experimental import pallas as pl
from jax.experimental.pallas import tpu as pltpu
from jax.sharding import PartitionSpec as P

MESH = pl.DeviceIdType.MESH
F32 = jnp.float32
BF16 = jnp.bfloat16


def split_table(table):
    table = np.asarray(table, np.float32)
    high = table.astype(jnp.bfloat16)
    low = (table - high.astype(np.float32)).astype(jnp.bfloat16)
    return high, low


def make_tables(n):
    line = np.arange(n, dtype=np.float64)
    turn = 2.0 * np.pi
    angle_one = turn * np.outer(line + 0.25, line) / n
    angle_mid = turn * np.outer(line + 0.25, line) / (n * n)
    angle_two = turn * (np.outer(line, line) % n) / n
    cos_one, sin_one = np.cos(angle_one), np.sin(angle_one)
    cos_two, sin_two = np.cos(angle_two), np.sin(angle_two)
    first_hi, first_lo = split_table(np.concatenate([cos_one, -sin_one], 0))
    first = np.concatenate([first_hi, first_lo], 1)
    fwd_hi, fwd_lo = split_table(np.block([[cos_two, -sin_two], [sin_two, cos_two]]))
    inv_hi, inv_lo = split_table(np.block([[cos_two, sin_two], [-sin_two, cos_two]]))
    last_hi, last_lo = split_table(np.concatenate([cos_one.T, -sin_one.T], 1))
    last = np.concatenate([last_hi, last_lo], 0)
    pick = np.zeros((256, 256), np.float32)
    for dest in range(32):
        for row in range(4):
            part, at = row // 2, row % 2
            pick[128 * part + 4 * dest + at, 4 * dest + row] = 1.0
            pick[128 * part + 4 * dest + 2 + at, 128 + 4 * dest + row] = 1.0
    wide = np.stack([first, fwd_hi, fwd_lo, inv_hi, inv_lo, last, pick.astype(jnp.bfloat16)])
    eye = np.eye(n, dtype=np.float32).astype(jnp.bfloat16)
    mid = np.stack([np.cos(angle_mid), np.sin(angle_mid)]).astype(np.float32)
    return wide, eye, mid


def mm(a, b):
    return jnp.dot(a, b, preferred_element_type=F32)


def mm_t(a, b):
    return lax.dot_general(a, b, (((1,), (1,)), ((), ())), preferred_element_type=F32)


def split(x):
    high = x.astype(BF16)
    return high, (x - high.astype(F32)).astype(BF16)


def kernel(
    dims,
    vals_hbm,
    gate_hbm,
    grad_hbm,
    filt_hbm,
    skip_hbm,
    wide_hbm,
    mid_hbm,
    home_ref,
    whole_ref,
    vals_ref,
    gate_ref,
    grad_ref,
    filt_ref,
    skip_ref,
    wide_ref,
    mid_ref,
    out_box,
    in_box,
    back_box,
    rows,
    hspec,
    spec,
    own,
    cross,
    parts,
    total,
    load_sems,
    sems,
    arrived,
    returned,
    ready,
):
    n, seqs, nx, nz, ny, nc = dims
    ctx = n
    chans = 4
    me = lax.axis_index("ctx")
    my_seq = lax.axis_index("dp")

    loads = []
    for i, (src, dst) in enumerate(
        (
            (grad_hbm, grad_ref),
            (gate_hbm, gate_ref),
            (vals_hbm, vals_ref),
            (wide_hbm, wide_ref),
            (filt_hbm, filt_ref),
            (mid_hbm, mid_ref),
            (skip_hbm, skip_ref),
        )
    ):
        loads.append(pltpu.make_async_copy(src, dst, load_sems.at[i]))
        loads[-1].start()

    my_c = lax.rem(me, nc)
    my_y = lax.rem(me // nc, ny)
    my_z = lax.rem(me // (nc * ny), nz)
    my_x = me // (nc * ny * nz)
    x_part = [lax.rem(my_x + d, nx) * (nz * ny * nc) for d in range(nx)]
    z_part = [lax.rem(my_z + d, nz) * (ny * nc) for d in range(nz)]
    c_part = [lax.rem(my_c + d, nc) for d in range(nc)]
    lines = [x + z + c for x in x_part for z in z_part for c in c_part]

    def each_peer(visit):
        def plane(step, carry):
            y = lax.rem(my_y + step, ny) * nc
            for line in lines:
                visit(line + y)
            return carry

        lax.fori_loop(ny // 2, ny, plane, 0)
        lax.fori_loop(1, ny // 2, plane, 0)
        for line in lines[1:]:
            visit(line + my_y * nc)

    barrier = pltpu.get_barrier_semaphore()

    def greet(peer):
        pl.semaphore_signal(
            barrier, inc=1, device_id=(my_seq, peer), device_id_type=MESH
        )

    each_peer(greet)
    others = [lax.rem(my_seq + d, seqs) for d in range(seqs)]
    for d in range(1, seqs):

        @pl.when(my_seq + d < seqs)
        def _(d=d):
            pl.semaphore_signal(
                barrier, inc=1, device_id=(others[d], me), device_id_type=MESH
            )

    for load in loads[:4]:
        load.wait()
    first, fwd_hi, fwd_lo = wide_ref[0], wide_ref[1], wide_ref[2]
    inv_hi, inv_lo, last, pick = wide_ref[3], wide_ref[4], wide_ref[5], wide_ref[6]

    for g in range(chans):
        cols = slice(128 * g, 128 * (g + 1))
        gated = (grad_ref[:, cols].astype(F32) * gate_ref[:, cols].astype(F32)).astype(BF16)
        both = jnp.concatenate([vals_ref[:, cols], gated], 1)
        mail = mm_t(pick, both).astype(BF16)
        for part in range(2):
            out_box[part, 32 * g : 32 * (g + 1)] = mail[n * part : n * (part + 1)].reshape(32, 4, n)

    pl.semaphore_wait(barrier, ctx - 1 + my_seq)

    def exchange(src, dst, send_sem, recv_sem):
        def send(peer):
            pltpu.make_async_remote_copy(
                src_ref=src.at[peer],
                dst_ref=dst.at[me],
                send_sem=send_sem,
                recv_sem=recv_sem,
                device_id=(my_seq, peer),
                device_id_type=MESH,
            ).start()

        each_peer(send)
        pltpu.make_async_copy(src.at[me], dst.at[me], recv_sem).start()

    def drain(box, sem, count):
        part = box.at[pl.ds(0, count)]
        pltpu.make_async_copy(part, part, sem).wait()

    for part in range(2):
        exchange(out_box.at[part], in_box.at[part], sems.at[part], arrived.at[part])
    for d in range(1, seqs):

        @pl.when(my_seq + d >= seqs)
        def _(d=d):
            pl.semaphore_signal(
                ready, inc=1, device_id=(others[d], me), device_id_type=MESH
            )

    for load in loads[4:]:
        load.wait()
    cos_mid, sin_mid = mid_ref[0], mid_ref[1]

    def forward(blocks, exact):
        count = len(blocks)
        data = jnp.concatenate(blocks, 1)
        if exact:
            data = data.astype(BF16)
            part = mm(first, jnp.concatenate([data, data], 0))
        else:
            high, low = split(data)
            part = mm(first, jnp.concatenate([high, high], 0)) + mm(first[:, :n], low)
        turned = []
        for i in range(count):
            re = part[:n, n * i : n * (i + 1)]
            im = part[n:, n * i : n * (i + 1)]
            turned.append(
                jnp.concatenate([re * cos_mid + im * sin_mid, im * cos_mid - re * sin_mid], 1)
            )
        high, low = split(jnp.concatenate(turned, 0))
        return mm(high, fwd_hi) + (mm(low, fwd_hi) + mm(high, fwd_lo))

    def inverse(re, im):
        high, low = split(jnp.concatenate([re, im], 1))
        part = mm(high, inv_hi) + (mm(low, inv_hi) + mm(high, inv_lo))
        res, ims = [], []
        for i in range(part.shape[0] // n):
            re = part[n * i : n * (i + 1), :n]
            im = part[n * i : n * (i + 1), n:]
            res.append(re * cos_mid - im * sin_mid)
            ims.append(im * cos_mid + re * sin_mid)
        high, low = split(
            jnp.concatenate([jnp.concatenate(res, 1), jnp.concatenate(ims, 1)], 0)
        )
        both = mm(last, high)
        return both[:n] + (both[n:] + mm(last[:n], low))

    scale = float(n) ** -1
    unit = float(n) ** -2
    h = forward([filt_ref[pl.ds(c, n, stride=chans), :] for c in range(chans)], False)
    for c in range(chans):
        band = slice(n * c, n * (c + 1))
        hspec[band, :n] = (h[band, :n] * scale + skip_ref[c]) * unit
        hspec[band, n:] = h[band, n:] * (scale * unit)

    early = my_seq < seqs // 2
    far_first = sorted(range(1, seqs), key=lambda d: -min(d, seqs - d))
    pair = 2 * n

    def send_parts(channels):
        for d in far_first:

            @pl.when(others[d] // 2 == channels)
            def _(d=d):
                pltpu.make_async_remote_copy(
                    src_ref=cross.at[others[d]],
                    dst_ref=parts.at[d - 1],
                    send_sem=sems.at[4],
                    recv_sem=sems.at[5],
                    device_id=(others[d], me),
                    device_id_type=MESH,
                ).start()

    def wait_ready():
        @pl.when(my_seq < seqs - 1)
        def _():
            pl.semaphore_wait(ready, seqs - 1 - my_seq)

    def send_back(part):
        v_re, v_im = spec[part, :pair, :n], spec[part, :pair, n:]
        d_re, d_im = spec[part, pair:, :n], spec[part, pair:, n:]
        band = slice(pair * part, pair * (part + 1))
        h_re, h_im = hspec[band, :n], hspec[band, n:]
        conv = inverse(h_re * v_re - h_im * v_im, h_re * v_im + h_im * v_re)
        gval = inverse(h_re * d_re + h_im * d_im, h_re * d_im - h_im * d_re)
        for c in range(2):
            rows[pl.ds(c, n, stride=4), :] = conv[:, n * c : n * (c + 1)]
            rows[pl.ds(2 + c, n, stride=4), :] = gval[:, n * c : n * (c + 1)]
        back_box[part] = rows[...].reshape(n, 4, n).astype(BF16)
        exchange(back_box.at[part], home_ref.at[part], sems.at[2 + part], returned.at[part])

    for part in range(2):
        pltpu.make_async_copy(in_box.at[part], in_box.at[part], arrived.at[part]).wait()
        rows[...] = in_box[part].astype(F32).reshape(4 * n, n)
        spec[part] = forward([rows[pl.ds(c, n, stride=4), :] for c in range(4)], True)
        v_re, v_im = spec[part, :pair, :n], spec[part, :pair, n:]
        d_re, d_im = spec[part, pair:, :n], spec[part, pair:, n:]
        lag = inverse(d_re * v_re + d_im * v_im, d_im * v_re - d_re * v_im)
        lag = lag * (unit * (seqs**-0.5) * scale)
        for c in range(2):
            own[2 * part + c] = lag[:, n * c : n * (c + 1)]
            cross[2 * part + c] = lag[:, n * c : n * (c + 1)].astype(BF16)
        if part == 0:

            @pl.when(jnp.logical_not(early))
            def _():
                wait_ready()
                send_parts(0)

        else:

            @pl.when(early)
            def _():
                wait_ready()
                send_parts(0)

            send_parts(1)

    @pl.when(early)
    def _():
        for part in range(2):
            send_back(part)

    drain(parts, sems.at[5], seqs - 1)
    summed = own[my_seq]
    for d in range(seqs - 1):
        summed = summed + parts[d].astype(F32)
    total[0] = summed.astype(BF16)
    for d in far_first:
        pltpu.make_async_remote_copy(
            src_ref=total.at[0],
            dst_ref=whole_ref.at[my_seq],
            send_sem=sems.at[6],
            recv_sem=sems.at[7],
            device_id=(others[d], me),
            device_id_type=MESH,
        ).start()
    pltpu.make_async_copy(total.at[0], whole_ref.at[my_seq], sems.at[7]).start()

    @pl.when(jnp.logical_not(early))
    def _():
        for part in range(2):
            send_back(part)

    for part in range(2):
        drain(out_box.at[part], sems.at[part], ctx - 1)
        drain(back_box.at[part], sems.at[2 + part], ctx - 1)
    drain(cross, sems.at[4], seqs - 1)
    drain(cross, sems.at[6], seqs - 1)
    for part in range(2):
        drain(home_ref.at[part], returned.at[part], ctx)
    drain(whole_ref, sems.at[7], seqs)


def finish(home_ref, whole_ref, grad_ref, pick_ref, eye_ref, gval_ref, ggate_ref, gfilt_ref):
    n = grad_ref.shape[0]
    chans = whole_ref.shape[0]
    pick = pick_ref[...]
    for c in range(chans):
        gfilt_ref[pl.ds(c, n, stride=chans), :] = whole_ref[c].astype(F32)
    for g in range(chans):
        cols = slice(128 * g, 128 * (g + 1))
        group = jnp.concatenate(
            [home_ref[part, 32 * g : 32 * (g + 1)].reshape(128, n) for part in range(2)], 0
        )
        both = mm(mm_t(eye_ref[...], group).astype(BF16), pick)
        gval_ref[:, cols] = both[:, n:].astype(BF16)
        ggate_ref[:, cols] = (grad_ref[:, cols].astype(F32) * both[:, :n]).astype(BF16)


def per_device(sizes, values, gates, grad_out, filters, skip):
    seqs, ctx = sizes
    length = filters.shape[1]
    n = values.shape[1]
    chans = filters.shape[0]
    wide, eye, mid = (jnp.asarray(t) for t in make_tables(n))
    pick = jnp.asarray(make_tables(n)[0][6])
    filt = filters.reshape(chans, n, n).transpose(1, 0, 2).reshape(n * chans, n)
    vmem = pl.BlockSpec(memory_space=pltpu.VMEM)
    anywhere = pl.BlockSpec(memory_space=pl.ANY)
    in_hbm = pl.BlockSpec(memory_space=pltpu.HBM)
    home, whole = pl.pallas_call(
        functools.partial(kernel, (n, seqs, 4, 2, 8, 2)),
        name="hyena_bwd",
        out_shape=(
            pltpu.VMEM((2, n, 4, n), BF16),
            pltpu.VMEM((seqs, n, n), BF16),
        ),
        in_specs=[in_hbm] * 7,
        out_specs=(anywhere,) * 2,
        scratch_shapes=[
            pltpu.VMEM((n, chans * n), BF16),
            pltpu.VMEM((n, chans * n), BF16),
            pltpu.VMEM((n, chans * n), BF16),
            pltpu.VMEM((n * chans, n), F32),
            pltpu.SMEM((chans,), F32),
            pltpu.VMEM(wide.shape, BF16),
            pltpu.VMEM(mid.shape, F32),
            pltpu.VMEM((2, n, 4, n), BF16),
            pltpu.VMEM((2, n, 4, n), BF16),
            pltpu.VMEM((2, n, 4, n), BF16),
            pltpu.VMEM((4 * n, n), F32),
            pltpu.VMEM((chans * n, 2 * n), F32),
            pltpu.VMEM((2, chans * n, 2 * n), F32),
            pltpu.VMEM((chans, n, n), F32),
            pltpu.VMEM((chans, n, n), BF16),
            pltpu.VMEM((seqs - 1, n, n), BF16),
            pltpu.VMEM((1, n, n), BF16),
            pltpu.SemaphoreType.DMA((7,)),
            pltpu.SemaphoreType.DMA((8,)),
            pltpu.SemaphoreType.DMA((2,)),
            pltpu.SemaphoreType.DMA((2,)),
            pltpu.SemaphoreType.REGULAR,
        ],
        compiler_params=pltpu.CompilerParams(
            collective_id=0, has_side_effects=True, vmem_limit_bytes=60 * 1024 * 1024
        ),
    )(values[0], gates[0], grad_out[0], filt, skip, wide, mid)
    gval, ggate, gfilt = pl.pallas_call(
        finish,
        name="hyena_out",
        out_shape=(
            jax.ShapeDtypeStruct(values.shape[1:], BF16),
            jax.ShapeDtypeStruct(values.shape[1:], BF16),
            jax.ShapeDtypeStruct((n * chans, n), F32),
        ),
        in_specs=[vmem] * 5,
        out_specs=(vmem,) * 3,
        compiler_params=pltpu.CompilerParams(vmem_limit_bytes=8 << 20),
    )(home, whole, grad_out[0], pick, eye)
    gfilt = gfilt.reshape(n, chans, n).transpose(1, 0, 2).reshape(chans, length)
    return gval[None], ggate[None], gfilt


def solution(mesh):
    in_specs = (
        P("dp", "ctx", None),
        P("dp", "ctx", None),
        P("dp", "ctx", None),
        P("ctx", None),
        P("ctx"),
    )
    out_specs = (P("dp", "ctx", None), P("dp", "ctx", None), P("ctx", None))
    return jax.shard_map(
        functools.partial(per_device, (mesh.shape["dp"], mesh.shape["ctx"])),
        mesh=mesh,
        in_specs=in_specs,
        out_specs=out_specs,
        check_vma=False,
    )
```

```python
import functools

import jax
import jax.numpy as jnp
import numpy as np
from jax import lax
from jax.experimental import pallas as pl
from jax.experimental.pallas import tpu as pltpu
from jax.sharding import PartitionSpec as P

MESH = pl.DeviceIdType.MESH
F32 = jnp.float32
BF16 = jnp.bfloat16


def split_table(table):
    table = np.asarray(table, np.float32)
    high = table.astype(jnp.bfloat16)
    low = (table - high.astype(np.float32)).astype(jnp.bfloat16)
    return high, low


def make_tables(n):
    line = np.arange(n, dtype=np.float64)
    turn = 2.0 * np.pi
    angle_one = turn * np.outer(line + 0.25, line) / n
    angle_mid = turn * np.outer(line + 0.25, line) / (n * n)
    angle_two = turn * (np.outer(line, line) % n) / n
    cos_one, sin_one = np.cos(angle_one), np.sin(angle_one)
    cos_two, sin_two = np.cos(angle_two), np.sin(angle_two)
    first_hi, first_lo = split_table(np.concatenate([cos_one, -sin_one], 0))
    first = np.concatenate([first_hi, first_lo], 1)
    fwd_hi, fwd_lo = split_table(np.block([[cos_two, -sin_two], [sin_two, cos_two]]))
    inv_hi, inv_lo = split_table(np.block([[cos_two, sin_two], [-sin_two, cos_two]]))
    last_hi, last_lo = split_table(np.concatenate([cos_one.T, -sin_one.T], 1))
    last = np.concatenate([last_hi, last_lo], 0)
    pick = np.zeros((256, 256), np.float32)
    for dest in range(32):
        for row in range(4):
            part, at = row // 2, row % 2
            pick[128 * part + 4 * dest + at, 4 * dest + row] = 1.0
            pick[128 * part + 4 * dest + 2 + at, 128 + 4 * dest + row] = 1.0
    wide = np.stack([first, fwd_hi, fwd_lo, inv_hi, inv_lo, last, pick.astype(jnp.bfloat16)])
    eye = np.eye(n, dtype=np.float32).astype(jnp.bfloat16)
    mid = np.stack([np.cos(angle_mid), np.sin(angle_mid)]).astype(np.float32)
    return wide, eye, mid


def mm(a, b):
    return jnp.dot(a, b, preferred_element_type=F32)


def mm_t(a, b):
    return lax.dot_general(a, b, (((1,), (1,)), ((), ())), preferred_element_type=F32)


def split(x):
    high = x.astype(BF16)
    return high, (x - high.astype(F32)).astype(BF16)


def kernel(
    dims,
    vals_hbm,
    gate_hbm,
    grad_hbm,
    filt_hbm,
    skip_hbm,
    wide_hbm,
    mid_hbm,
    eye_hbm,
    gval_ref,
    ggate_ref,
    whole_ref,
    vals_ref,
    gate_ref,
    grad_ref,
    filt_ref,
    skip_ref,
    wide_ref,
    mid_ref,
    eye_ref,
    out_box,
    in_box,
    back_box,
    home_ref,
    rows,
    hspec,
    spec,
    own,
    cross,
    parts,
    total,
    load_sems,
    sems,
    arrived,
    returned,
    ready,
):
    n, seqs, nx, nz, ny, nc = dims
    ctx = n
    chans = 4
    me = lax.axis_index("ctx")
    my_seq = lax.axis_index("dp")

    loads = []
    for i, (src, dst) in enumerate(
        (
            (grad_hbm, grad_ref),
            (gate_hbm, gate_ref),
            (vals_hbm, vals_ref),
            (wide_hbm, wide_ref),
            (filt_hbm, filt_ref),
            (mid_hbm, mid_ref),
            (skip_hbm, skip_ref),
            (eye_hbm, eye_ref),
        )
    ):
        loads.append(pltpu.make_async_copy(src, dst, load_sems.at[i]))
        loads[-1].start()

    my_c = lax.rem(me, nc)
    my_y = lax.rem(me // nc, ny)
    my_z = lax.rem(me // (nc * ny), nz)
    my_x = me // (nc * ny * nz)
    x_part = [lax.rem(my_x + d, nx) * (nz * ny * nc) for d in range(nx)]
    z_part = [lax.rem(my_z + d, nz) * (ny * nc) for d in range(nz)]
    c_part = [lax.rem(my_c + d, nc) for d in range(nc)]
    x_far = sorted(range(nx), key=lambda d: -min(d, nx - d))
    lines = [x_part[d] + z + c for d in x_far for z in z_part[::-1] for c in c_part[::-1]]

    def each_peer(visit):
        def planes(step, carry):
            up = lax.rem(my_y + (ny // 2 - step), ny) * nc
            down = lax.rem(my_y + (ny // 2 + step), ny) * nc
            for line in lines:
                visit(line + up)
                visit(line + down)
            return carry

        across = lax.rem(my_y + ny // 2, ny) * nc
        for line in lines:
            visit(line + across)
        lax.fori_loop(1, ny // 2, planes, 0)
        for line in lines[:-1]:
            visit(line + my_y * nc)

    barrier = pltpu.get_barrier_semaphore()

    def greet(peer):
        pl.semaphore_signal(
            barrier, inc=1, device_id=(my_seq, peer), device_id_type=MESH
        )

    each_peer(greet)
    others = [lax.rem(my_seq + d, seqs) for d in range(seqs)]
    for d in range(1, seqs):

        @pl.when(my_seq + d < seqs)
        def _(d=d):
            pl.semaphore_signal(
                barrier, inc=1, device_id=(others[d], me), device_id_type=MESH
            )

    for load in loads[:4]:
        load.wait()
    first, fwd_hi, fwd_lo = wide_ref[0], wide_ref[1], wide_ref[2]
    inv_hi, inv_lo, last, pick = wide_ref[3], wide_ref[4], wide_ref[5], wide_ref[6]

    for g in range(chans):
        cols = slice(128 * g, 128 * (g + 1))
        gated = (grad_ref[:, cols].astype(F32) * gate_ref[:, cols].astype(F32)).astype(BF16)
        both = jnp.concatenate([vals_ref[:, cols], gated], 1)
        mail = mm_t(pick, both).astype(BF16)
        for part in range(2):
            out_box[part, 32 * g : 32 * (g + 1)] = mail[n * part : n * (part + 1)].reshape(32, 4, n)

    pl.semaphore_wait(barrier, ctx - 1 + my_seq)

    def exchange(src, dst, send_sem, recv_sem):
        def send(peer):
            pltpu.make_async_remote_copy(
                src_ref=src.at[peer],
                dst_ref=dst.at[me],
                send_sem=send_sem,
                recv_sem=recv_sem,
                device_id=(my_seq, peer),
                device_id_type=MESH,
            ).start()

        each_peer(send)
        pltpu.make_async_copy(src.at[me], dst.at[me], recv_sem).start()

    def drain(box, sem, count):
        part = box.at[pl.ds(0, count)]
        pltpu.make_async_copy(part, part, sem).wait()

    for part in range(2):
        exchange(out_box.at[part], in_box.at[part], sems.at[part], arrived.at[part])
    for d in range(1, seqs):

        @pl.when(my_seq + d >= seqs)
        def _(d=d):
            pl.semaphore_signal(
                ready, inc=1, device_id=(others[d], me), device_id_type=MESH
            )

    for load in loads[4:]:
        load.wait()
    cos_mid, sin_mid = mid_ref[0], mid_ref[1]

    def forward(blocks, exact):
        count = len(blocks)
        data = jnp.concatenate(blocks, 1)
        if exact:
            data = data.astype(BF16)
            part = mm(first, jnp.concatenate([data, data], 0))
        else:
            high, low = split(data)
            part = mm(first, jnp.concatenate([high, high], 0)) + mm(first[:, :n], low)
        turned = []
        for i in range(count):
            re = part[:n, n * i : n * (i + 1)]
            im = part[n:, n * i : n * (i + 1)]
            turned.append(
                jnp.concatenate([re * cos_mid + im * sin_mid, im * cos_mid - re * sin_mid], 1)
            )
        high, low = split(jnp.concatenate(turned, 0))
        return mm(high, fwd_hi) + (mm(low, fwd_hi) + mm(high, fwd_lo))

    def inverse(re, im):
        high, low = split(jnp.concatenate([re, im], 1))
        part = mm(high, inv_hi) + (mm(low, inv_hi) + mm(high, inv_lo))
        res, ims = [], []
        for i in range(part.shape[0] // n):
            re = part[n * i : n * (i + 1), :n]
            im = part[n * i : n * (i + 1), n:]
            res.append(re * cos_mid - im * sin_mid)
            ims.append(im * cos_mid + re * sin_mid)
        high, low = split(
            jnp.concatenate([jnp.concatenate(res, 1), jnp.concatenate(ims, 1)], 0)
        )
        both = mm(last, high)
        return both[:n] + (both[n:] + mm(last[:n], low))

    scale = float(n) ** -1
    unit = float(n) ** -2
    h = forward([filt_ref[pl.ds(c, n, stride=chans), :] for c in range(chans)], False)
    for c in range(chans):
        band = slice(n * c, n * (c + 1))
        hspec[band, :n] = (h[band, :n] * scale + skip_ref[c]) * unit
        hspec[band, n:] = h[band, n:] * (scale * unit)

    early = my_seq < seqs // 2
    far_first = sorted(range(1, seqs), key=lambda d: -min(d, seqs - d))
    pair = 2 * n

    def send_parts(channels):
        for d in far_first:

            @pl.when(others[d] // 2 == channels)
            def _(d=d):
                pltpu.make_async_remote_copy(
                    src_ref=cross.at[others[d]],
                    dst_ref=parts.at[d - 1],
                    send_sem=sems.at[4],
                    recv_sem=sems.at[5],
                    device_id=(others[d], me),
                    device_id_type=MESH,
                ).start()

    def wait_ready():
        @pl.when(my_seq < seqs - 1)
        def _():
            pl.semaphore_wait(ready, seqs - 1 - my_seq)

    def results_of(part):
        v_re, v_im = spec[part, :pair, :n], spec[part, :pair, n:]
        d_re, d_im = spec[part, pair:, :n], spec[part, pair:, n:]
        band = slice(pair * part, pair * (part + 1))
        h_re, h_im = hspec[band, :n], hspec[band, n:]
        conv = inverse(h_re * v_re - h_im * v_im, h_re * v_im + h_im * v_re)
        gval = inverse(h_re * d_re + h_im * d_im, h_re * d_im - h_im * d_re)
        for c in range(2):
            rows[pl.ds(c, n, stride=4), :] = conv[:, n * c : n * (c + 1)]
            rows[pl.ds(2 + c, n, stride=4), :] = gval[:, n * c : n * (c + 1)]
        back_box[part] = rows[...].reshape(n, 4, n).astype(BF16)

    def send_back(part):
        exchange(back_box.at[part], home_ref.at[part], sems.at[2 + part], returned.at[part])

    for part in range(2):
        pltpu.make_async_copy(in_box.at[part], in_box.at[part], arrived.at[part]).wait()
        rows[...] = in_box[part].astype(F32).reshape(4 * n, n)
        spec[part] = forward([rows[pl.ds(c, n, stride=4), :] for c in range(4)], True)
        v_re, v_im = spec[part, :pair, :n], spec[part, :pair, n:]
        d_re, d_im = spec[part, pair:, :n], spec[part, pair:, n:]
        lag = inverse(d_re * v_re + d_im * v_im, d_im * v_re - d_re * v_im)
        lag = lag * (unit * (seqs**-0.5) * scale)
        for c in range(2):
            own[2 * part + c] = lag[:, n * c : n * (c + 1)]
            cross[2 * part + c] = lag[:, n * c : n * (c + 1)].astype(BF16)
        if part == 0:

            @pl.when(jnp.logical_not(early))
            def _():
                wait_ready()
                send_parts(0)

        else:

            @pl.when(early)
            def _():
                wait_ready()
                send_parts(0)

            send_parts(1)

    for part in range(2):
        results_of(part)

        @pl.when(early)
        def _(part=part):
            send_back(part)

    drain(parts, sems.at[5], seqs - 1)
    summed = own[my_seq]
    for d in range(seqs - 1):
        summed = summed + parts[d].astype(F32)
    total[0] = summed.astype(BF16)
    for d in far_first:
        pltpu.make_async_remote_copy(
            src_ref=total.at[0],
            dst_ref=whole_ref.at[my_seq],
            send_sem=sems.at[6],
            recv_sem=sems.at[7],
            device_id=(others[d], me),
            device_id_type=MESH,
        ).start()
    pltpu.make_async_copy(total.at[0], whole_ref.at[my_seq], sems.at[7]).start()

    @pl.when(jnp.logical_not(early))
    def _():
        for part in range(2):
            send_back(part)

    for part in range(2):
        drain(out_box.at[part], sems.at[part], ctx - 1)
        drain(back_box.at[part], sems.at[2 + part], ctx - 1)
    drain(cross, sems.at[4], seqs - 1)
    drain(cross, sems.at[6], seqs - 1)
    for part in range(2):
        drain(home_ref.at[part], returned.at[part], ctx)
    for g in range(chans):
        cols = slice(128 * g, 128 * (g + 1))
        group = jnp.concatenate(
            [home_ref[part, 32 * g : 32 * (g + 1)].reshape(128, n) for part in range(2)], 0
        )
        both = mm(mm_t(eye_ref[...], group).astype(BF16), pick)
        gval_ref[:, cols] = both[:, n:].astype(BF16)
        ggate_ref[:, cols] = (grad_ref[:, cols].astype(F32) * both[:, :n]).astype(BF16)
    drain(whole_ref, sems.at[7], seqs)


def finish(gval_in, ggate_in, whole_ref, gval_hbm, ggate_hbm, gfilt_hbm, gfilt_ref, sems):
    seqs, n = whole_ref.shape[:2]
    copies = [
        pltpu.make_async_copy(gval_in, gval_hbm, sems.at[0]),
        pltpu.make_async_copy(ggate_in, ggate_hbm, sems.at[1]),
        pltpu.make_async_copy(gfilt_ref, gfilt_hbm, sems.at[2]),
    ]
    copies[0].start()
    copies[1].start()
    for c in range(seqs):
        gfilt_ref[pl.ds(c, n, stride=seqs), :] = whole_ref[c].astype(F32)
    copies[2].start()
    for copy in copies:
        copy.wait()


def per_device(sizes, values, gates, grad_out, filters, skip):
    seqs, ctx = sizes
    length = filters.shape[1]
    n = values.shape[1]
    chans = filters.shape[0]
    wide, eye, mid = (jnp.asarray(t) for t in make_tables(n))
    filt = filters.reshape(chans, n, n).transpose(1, 0, 2).reshape(n * chans, n)
    vmem = pl.BlockSpec(memory_space=pltpu.VMEM)
    anywhere = pl.BlockSpec(memory_space=pl.ANY)
    in_hbm = pl.BlockSpec(memory_space=pltpu.HBM)
    gval, ggate, whole = pl.pallas_call(
        functools.partial(kernel, (n, seqs, 4, 2, 8, 2)),
        name="hyena_bwd",
        out_shape=(
            pltpu.VMEM((n, chans * n), BF16),
            pltpu.VMEM((n, chans * n), BF16),
            pltpu.VMEM((seqs, n, n), BF16),
        ),
        in_specs=[in_hbm] * 8,
        out_specs=(vmem, vmem, anywhere),
        scratch_shapes=[
            pltpu.VMEM((n, chans * n), BF16),
            pltpu.VMEM((n, chans * n), BF16),
            pltpu.VMEM((n, chans * n), BF16),
            pltpu.VMEM((n * chans, n), F32),
            pltpu.SMEM((chans,), F32),
            pltpu.VMEM(wide.shape, BF16),
            pltpu.VMEM(mid.shape, F32),
            pltpu.VMEM(eye.shape, BF16),
            pltpu.VMEM((2, n, 4, n), BF16),
            pltpu.VMEM((2, n, 4, n), BF16),
            pltpu.VMEM((2, n, 4, n), BF16),
            pltpu.VMEM((2, n, 4, n), BF16),
            pltpu.VMEM((4 * n, n), F32),
            pltpu.VMEM((chans * n, 2 * n), F32),
            pltpu.VMEM((2, chans * n, 2 * n), F32),
            pltpu.VMEM((chans, n, n), F32),
            pltpu.VMEM((chans, n, n), BF16),
            pltpu.VMEM((seqs - 1, n, n), BF16),
            pltpu.VMEM((1, n, n), BF16),
            pltpu.SemaphoreType.DMA((8,)),
            pltpu.SemaphoreType.DMA((8,)),
            pltpu.SemaphoreType.DMA((2,)),
            pltpu.SemaphoreType.DMA((2,)),
            pltpu.SemaphoreType.REGULAR,
        ],
        compiler_params=pltpu.CompilerParams(
            collective_id=0, has_side_effects=True, vmem_limit_bytes=60 * 1024 * 1024
        ),
    )(values[0], gates[0], grad_out[0], filt, skip, wide, mid, eye)
    gval, ggate, gfilt = pl.pallas_call(
        finish,
        name="hyena_out",
        out_shape=(
            jax.ShapeDtypeStruct(values.shape[1:], BF16),
            jax.ShapeDtypeStruct(values.shape[1:], BF16),
            jax.ShapeDtypeStruct((n * chans, n), F32),
        ),
        in_specs=[vmem] * 3,
        out_specs=(in_hbm,) * 3,
        scratch_shapes=[
            pltpu.VMEM((n * chans, n), F32),
            pltpu.SemaphoreType.DMA((3,)),
        ],
        compiler_params=pltpu.CompilerParams(vmem_limit_bytes=8 << 20),
    )(gval, ggate, whole)
    gfilt = gfilt.reshape(n, chans, n).transpose(1, 0, 2).reshape(chans, length)
    return gval[None], ggate[None], gfilt


def solution(mesh):
    in_specs = (
        P("dp", "ctx", None),
        P("dp", "ctx", None),
        P("dp", "ctx", None),
        P("ctx", None),
        P("ctx"),
    )
    out_specs = (P("dp", "ctx", None), P("dp", "ctx", None), P("ctx", None))
    return jax.shard_map(
        functools.partial(per_device, (mesh.shape["dp"], mesh.shape["ctx"])),
        mesh=mesh,
        in_specs=in_specs,
        out_specs=out_specs,
        check_vma=False,
    )
```

```python
import functools

import jax
import jax.numpy as jnp
import numpy as np
from jax import lax
from jax.experimental import pallas as pl
from jax.experimental.pallas import tpu as pltpu
from jax.sharding import PartitionSpec as P

MESH = pl.DeviceIdType.MESH
F32 = jnp.float32
BF16 = jnp.bfloat16


def split_table(table):
    table = np.asarray(table, np.float32)
    high = table.astype(jnp.bfloat16)
    low = (table - high.astype(np.float32)).astype(jnp.bfloat16)
    return high, low


def make_tables(n):
    line = np.arange(n, dtype=np.float64)
    turn = 2.0 * np.pi
    angle_one = turn * np.outer(line + 0.25, line) / n
    angle_mid = turn * np.outer(line + 0.25, line) / (n * n)
    angle_two = turn * (np.outer(line, line) % n) / n
    cos_one, sin_one = np.cos(angle_one), np.sin(angle_one)
    cos_two, sin_two = np.cos(angle_two), np.sin(angle_two)
    first_hi, first_lo = split_table(np.concatenate([cos_one, -sin_one], 0))
    first = np.concatenate([first_hi, first_lo], 1)
    fwd_hi, fwd_lo = split_table(np.block([[cos_two, -sin_two], [sin_two, cos_two]]))
    inv_hi, inv_lo = split_table(np.block([[cos_two, sin_two], [-sin_two, cos_two]]))
    last_hi, last_lo = split_table(np.concatenate([cos_one.T, -sin_one.T], 1))
    last = np.concatenate([last_hi, last_lo], 0)
    pick = np.zeros((256, 256), np.float32)
    for dest in range(32):
        for row in range(4):
            part, at = row // 2, row % 2
            pick[128 * part + 4 * dest + at, 4 * dest + row] = 1.0
            pick[128 * part + 4 * dest + 2 + at, 128 + 4 * dest + row] = 1.0
    wide = np.stack([first, fwd_hi, fwd_lo, inv_hi, inv_lo, last, pick.astype(jnp.bfloat16)])
    eye = np.eye(n, dtype=np.float32).astype(jnp.bfloat16)
    mid = np.stack([np.cos(angle_mid), np.sin(angle_mid)]).astype(np.float32)
    return wide, eye, mid


def mm(a, b):
    return jnp.dot(a, b, preferred_element_type=F32)


def mm_t(a, b):
    return lax.dot_general(a, b, (((1,), (1,)), ((), ())), preferred_element_type=F32)


def split(x):
    high = x.astype(BF16)
    return high, (x - high.astype(F32)).astype(BF16)


def kernel(
    dims,
    vals_hbm,
    gate_hbm,
    grad_hbm,
    filt_hbm,
    skip_hbm,
    wide_hbm,
    mid_hbm,
    eye_hbm,
    gval_ref,
    ggate_ref,
    whole_ref,
    vals_ref,
    gate_ref,
    grad_ref,
    filt_ref,
    skip_ref,
    wide_ref,
    mid_ref,
    eye_ref,
    out_box,
    in_box,
    back_box,
    home_ref,
    rows,
    hspec,
    spec,
    own,
    cross,
    parts,
    total,
    load_sems,
    sems,
    arrived,
    returned,
    ready,
):
    n, seqs, nx, nz, ny, nc = dims
    ctx = n
    chans = 4
    me = lax.axis_index("ctx")
    my_seq = lax.axis_index("dp")

    loads = []
    for i, (src, dst) in enumerate(
        (
            (grad_hbm, grad_ref),
            (gate_hbm, gate_ref),
            (vals_hbm, vals_ref),
            (wide_hbm, wide_ref),
            (filt_hbm, filt_ref),
            (mid_hbm, mid_ref),
            (skip_hbm, skip_ref),
            (eye_hbm, eye_ref),
        )
    ):
        loads.append(pltpu.make_async_copy(src, dst, load_sems.at[i]))
        loads[-1].start()

    my_c = lax.rem(me, nc)
    my_y = lax.rem(me // nc, ny)
    my_z = lax.rem(me // (nc * ny), nz)
    my_x = me // (nc * ny * nz)
    x_part = [lax.rem(my_x + d, nx) * (nz * ny * nc) for d in range(nx)]
    z_part = [lax.rem(my_z + d, nz) * (ny * nc) for d in range(nz)]
    c_part = [lax.rem(my_c + d, nc) for d in range(nc)]
    x_far = sorted(range(nx), key=lambda d: -min(d, nx - d))
    lines = [x_part[d] + z + c for d in x_far for z in z_part[::-1] for c in c_part[::-1]]

    def each_peer(visit):
        def planes(step, carry):
            up = lax.rem(my_y + (ny // 2 - step), ny) * nc
            down = lax.rem(my_y + (ny // 2 + step), ny) * nc
            for line in lines:
                visit(line + up)
                visit(line + down)
            return carry

        across = lax.rem(my_y + ny // 2, ny) * nc
        for line in lines:
            visit(line + across)
        lax.fori_loop(1, ny // 2, planes, 0)
        for line in lines[:-1]:
            visit(line + my_y * nc)

    barrier = pltpu.get_barrier_semaphore()

    def greet(peer):
        pl.semaphore_signal(
            barrier, inc=1, device_id=(my_seq, peer), device_id_type=MESH
        )

    each_peer(greet)
    others = [lax.rem(my_seq + d, seqs) for d in range(seqs)]
    for d in range(1, seqs):

        @pl.when(my_seq + d < seqs)
        def _(d=d):
            pl.semaphore_signal(
                barrier, inc=1, device_id=(others[d], me), device_id_type=MESH
            )

    for load in loads[:4]:
        load.wait()
    first, fwd_hi, fwd_lo = wide_ref[0], wide_ref[1], wide_ref[2]
    inv_hi, inv_lo, last, pick = wide_ref[3], wide_ref[4], wide_ref[5], wide_ref[6]

    for g in range(chans):
        cols = slice(128 * g, 128 * (g + 1))
        gated = (grad_ref[:, cols].astype(F32) * gate_ref[:, cols].astype(F32)).astype(BF16)
        both = jnp.concatenate([vals_ref[:, cols], gated], 1)
        mail = mm_t(pick, both).astype(BF16)
        for part in range(2):
            out_box[part, 32 * g : 32 * (g + 1)] = mail[n * part : n * (part + 1)].reshape(32, 4, n)

    pl.semaphore_wait(barrier, ctx - 1 + my_seq)

    def exchange(src, dst, send_sem, recv_sem):
        def send(peer):
            pltpu.make_async_remote_copy(
                src_ref=src.at[peer],
                dst_ref=dst.at[me],
                send_sem=send_sem,
                recv_sem=recv_sem,
                device_id=(my_seq, peer),
                device_id_type=MESH,
            ).start()

        each_peer(send)
        pltpu.make_async_copy(src.at[me], dst.at[me], recv_sem).start()

    def drain(box, sem, count):
        part = box.at[pl.ds(0, count)]
        pltpu.make_async_copy(part, part, sem).wait()

    for part in range(2):
        exchange(out_box.at[part], in_box.at[part], sems.at[part], arrived.at[part])
    for d in range(1, seqs):

        @pl.when(my_seq + d >= seqs)
        def _(d=d):
            pl.semaphore_signal(
                ready, inc=1, device_id=(others[d], me), device_id_type=MESH
            )

    for load in loads[4:]:
        load.wait()
    cos_mid, sin_mid = mid_ref[0], mid_ref[1]

    def forward(blocks, exact):
        count = len(blocks)
        data = jnp.concatenate(blocks, 1)
        if exact:
            data = data.astype(BF16)
            part = mm(first, jnp.concatenate([data, data], 0))
        else:
            high, low = split(data)
            part = mm(first, jnp.concatenate([high, high], 0)) + mm(first[:, :n], low)
        turned = []
        for i in range(count):
            re = part[:n, n * i : n * (i + 1)]
            im = part[n:, n * i : n * (i + 1)]
            turned.append(
                jnp.concatenate([re * cos_mid + im * sin_mid, im * cos_mid - re * sin_mid], 1)
            )
        high, low = split(jnp.concatenate(turned, 0))
        return mm(high, fwd_hi) + (mm(low, fwd_hi) + mm(high, fwd_lo))

    def inverse(re, im):
        high, low = split(jnp.concatenate([re, im], 1))
        part = mm(high, inv_hi) + (mm(low, inv_hi) + mm(high, inv_lo))
        res, ims = [], []
        for i in range(part.shape[0] // n):
            re = part[n * i : n * (i + 1), :n]
            im = part[n * i : n * (i + 1), n:]
            res.append(re * cos_mid - im * sin_mid)
            ims.append(im * cos_mid + re * sin_mid)
        high, low = split(
            jnp.concatenate([jnp.concatenate(res, 1), jnp.concatenate(ims, 1)], 0)
        )
        both = mm(last, high)
        return both[:n] + (both[n:] + mm(last[:n], low))

    scale = float(n) ** -1
    unit = float(n) ** -2
    h = forward([filt_ref[pl.ds(c, n, stride=chans), :] for c in range(chans)], False)
    for c in range(chans):
        band = slice(n * c, n * (c + 1))
        hspec[band, :n] = (h[band, :n] * scale + skip_ref[c]) * unit
        hspec[band, n:] = h[band, n:] * (scale * unit)

    early = my_seq < seqs // 2
    far_first = sorted(range(1, seqs), key=lambda d: -min(d, seqs - d))
    pair = 2 * n

    def send_parts(channels):
        for d in far_first:

            @pl.when(others[d] // 2 == channels)
            def _(d=d):
                pltpu.make_async_remote_copy(
                    src_ref=cross.at[others[d]],
                    dst_ref=parts.at[d - 1],
                    send_sem=sems.at[4],
                    recv_sem=sems.at[5],
                    device_id=(others[d], me),
                    device_id_type=MESH,
                ).start()

    def wait_ready():
        @pl.when(my_seq < seqs - 1)
        def _():
            pl.semaphore_wait(ready, seqs - 1 - my_seq)

    def results_of(part):
        v_re, v_im = spec[part, :pair, :n], spec[part, :pair, n:]
        d_re, d_im = spec[part, pair:, :n], spec[part, pair:, n:]
        band = slice(pair * part, pair * (part + 1))
        h_re, h_im = hspec[band, :n], hspec[band, n:]
        conv = inverse(h_re * v_re - h_im * v_im, h_re * v_im + h_im * v_re)
        gval = inverse(h_re * d_re + h_im * d_im, h_re * d_im - h_im * d_re)
        for c in range(2):
            rows[pl.ds(c, n, stride=4), :] = conv[:, n * c : n * (c + 1)]
            rows[pl.ds(2 + c, n, stride=4), :] = gval[:, n * c : n * (c + 1)]
        back_box[part] = rows[...].reshape(n, 4, n).astype(BF16)

    def send_back(part):
        exchange(back_box.at[part], home_ref.at[part], sems.at[2 + part], returned.at[part])

    for part in range(2):
        pltpu.make_async_copy(in_box.at[part], in_box.at[part], arrived.at[part]).wait()
        rows[...] = in_box[part].astype(F32).reshape(4 * n, n)
        spec[part] = forward([rows[pl.ds(c, n, stride=4), :] for c in range(4)], True)
        v_re, v_im = spec[part, :pair, :n], spec[part, :pair, n:]
        d_re, d_im = spec[part, pair:, :n], spec[part, pair:, n:]
        lag = inverse(d_re * v_re + d_im * v_im, d_im * v_re - d_re * v_im)
        lag = lag * (unit * (seqs**-0.5) * scale)
        for c in range(2):
            own[2 * part + c] = lag[:, n * c : n * (c + 1)]
            cross[2 * part + c] = lag[:, n * c : n * (c + 1)].astype(BF16)
        if part == 0:

            @pl.when(jnp.logical_not(early))
            def _():
                wait_ready()
                send_parts(0)

        else:

            @pl.when(early)
            def _():
                wait_ready()
                send_parts(0)

            send_parts(1)

    for part in range(2):
        results_of(part)

    @pl.when(early)
    def _():
        for part in range(2):
            send_back(part)

    drain(parts, sems.at[5], seqs - 1)
    summed = own[my_seq]
    for d in range(seqs - 1):
        summed = summed + parts[d].astype(F32)
    total[0] = summed.astype(BF16)
    for d in far_first:
        pltpu.make_async_remote_copy(
            src_ref=total.at[0],
            dst_ref=whole_ref.at[my_seq],
            send_sem=sems.at[6],
            recv_sem=sems.at[7],
            device_id=(others[d], me),
            device_id_type=MESH,
        ).start()
    pltpu.make_async_copy(total.at[0], whole_ref.at[my_seq], sems.at[7]).start()

    @pl.when(jnp.logical_not(early))
    def _():
        for part in range(2):
            send_back(part)

    for part in range(2):
        drain(out_box.at[part], sems.at[part], ctx - 1)
        drain(back_box.at[part], sems.at[2 + part], ctx - 1)
    drain(cross, sems.at[4], seqs - 1)
    drain(cross, sems.at[6], seqs - 1)
    for part in range(2):
        drain(home_ref.at[part], returned.at[part], ctx)
    for g in range(chans):
        cols = slice(128 * g, 128 * (g + 1))
        group = jnp.concatenate(
            [home_ref[part, 32 * g : 32 * (g + 1)].reshape(128, n) for part in range(2)], 0
        )
        both = mm(mm_t(eye_ref[...], group).astype(BF16), pick)
        gval_ref[:, cols] = both[:, n:].astype(BF16)
        ggate_ref[:, cols] = (grad_ref[:, cols].astype(F32) * both[:, :n]).astype(BF16)
    drain(whole_ref, sems.at[7], seqs)


def finish(gval_in, ggate_in, whole_ref, gval_hbm, ggate_hbm, gfilt_hbm, gfilt_ref, sems):
    seqs, n = whole_ref.shape[:2]
    copies = [
        pltpu.make_async_copy(gval_in, gval_hbm, sems.at[0]),
        pltpu.make_async_copy(ggate_in, ggate_hbm, sems.at[1]),
        pltpu.make_async_copy(gfilt_ref, gfilt_hbm, sems.at[2]),
    ]
    copies[0].start()
    copies[1].start()
    for c in range(seqs):
        gfilt_ref[pl.ds(c, n, stride=seqs), :] = whole_ref[c].astype(F32)
    copies[2].start()
    for copy in copies:
        copy.wait()


def per_device(sizes, values, gates, grad_out, filters, skip):
    seqs, ctx = sizes
    length = filters.shape[1]
    n = values.shape[1]
    chans = filters.shape[0]
    wide, eye, mid = (jnp.asarray(t) for t in make_tables(n))
    filt = filters.reshape(chans, n, n).transpose(1, 0, 2).reshape(n * chans, n)
    vmem = pl.BlockSpec(memory_space=pltpu.VMEM)
    anywhere = pl.BlockSpec(memory_space=pl.ANY)
    in_hbm = pl.BlockSpec(memory_space=pltpu.HBM)
    gval, ggate, whole = pl.pallas_call(
        functools.partial(kernel, (n, seqs, 4, 2, 8, 2)),
        name="hyena_bwd",
        out_shape=(
            pltpu.VMEM((n, chans * n), BF16),
            pltpu.VMEM((n, chans * n), BF16),
            pltpu.VMEM((seqs, n, n), BF16),
        ),
        in_specs=[in_hbm] * 8,
        out_specs=(vmem, vmem, anywhere),
        scratch_shapes=[
            pltpu.VMEM((n, chans * n), BF16),
            pltpu.VMEM((n, chans * n), BF16),
            pltpu.VMEM((n, chans * n), BF16),
            pltpu.VMEM((n * chans, n), F32),
            pltpu.SMEM((chans,), F32),
            pltpu.VMEM(wide.shape, BF16),
            pltpu.VMEM(mid.shape, F32),
            pltpu.VMEM(eye.shape, BF16),
            pltpu.VMEM((2, n, 4, n), BF16),
            pltpu.VMEM((2, n, 4, n), BF16),
            pltpu.VMEM((2, n, 4, n), BF16),
            pltpu.VMEM((2, n, 4, n), BF16),
            pltpu.VMEM((4 * n, n), F32),
            pltpu.VMEM((chans * n, 2 * n), F32),
            pltpu.VMEM((2, chans * n, 2 * n), F32),
            pltpu.VMEM((chans, n, n), F32),
            pltpu.VMEM((chans, n, n), BF16),
            pltpu.VMEM((seqs - 1, n, n), BF16),
            pltpu.VMEM((1, n, n), BF16),
            pltpu.SemaphoreType.DMA((8,)),
            pltpu.SemaphoreType.DMA((8,)),
            pltpu.SemaphoreType.DMA((2,)),
            pltpu.SemaphoreType.DMA((2,)),
            pltpu.SemaphoreType.REGULAR,
        ],
        compiler_params=pltpu.CompilerParams(
            collective_id=0, has_side_effects=True, vmem_limit_bytes=60 * 1024 * 1024
        ),
    )(values[0], gates[0], grad_out[0], filt, skip, wide, mid, eye)
    gval, ggate, gfilt = pl.pallas_call(
        finish,
        name="hyena_out",
        out_shape=(
            jax.ShapeDtypeStruct(values.shape[1:], BF16),
            jax.ShapeDtypeStruct(values.shape[1:], BF16),
            jax.ShapeDtypeStruct((n * chans, n), F32),
        ),
        in_specs=[vmem] * 3,
        out_specs=(in_hbm,) * 3,
        scratch_shapes=[
            pltpu.VMEM((n * chans, n), F32),
            pltpu.SemaphoreType.DMA((3,)),
        ],
        compiler_params=pltpu.CompilerParams(vmem_limit_bytes=8 << 20),
    )(gval, ggate, whole)
    gfilt = gfilt.reshape(n, chans, n).transpose(1, 0, 2).reshape(chans, length)
    return gval[None], ggate[None], gfilt


def solution(mesh):
    in_specs = (
        P("dp", "ctx", None),
        P("dp", "ctx", None),
        P("dp", "ctx", None),
        P("ctx", None),
        P("ctx"),
    )
    out_specs = (P("dp", "ctx", None), P("dp", "ctx", None), P("ctx", None))
    return jax.shard_map(
        functools.partial(per_device, (mesh.shape["dp"], mesh.shape["ctx"])),
        mesh=mesh,
        in_specs=in_specs,
        out_specs=out_specs,
        check_vma=False,
    )
```

```python
import functools

import jax
import jax.numpy as jnp
import numpy as np
from jax import lax
from jax.experimental import pallas as pl
from jax.experimental.pallas import tpu as pltpu
from jax.sharding import PartitionSpec as P

MESH = pl.DeviceIdType.MESH
F32 = jnp.float32
BF16 = jnp.bfloat16


def split_table(table):
    table = np.asarray(table, np.float32)
    high = table.astype(jnp.bfloat16)
    low = (table - high.astype(np.float32)).astype(jnp.bfloat16)
    return high, low


def make_tables(n):
    line = np.arange(n, dtype=np.float64)
    turn = 2.0 * np.pi
    angle_one = turn * np.outer(line + 0.25, line) / n
    angle_mid = turn * np.outer(line + 0.25, line) / (n * n)
    angle_two = turn * (np.outer(line, line) % n) / n
    cos_one, sin_one = np.cos(angle_one), np.sin(angle_one)
    cos_two, sin_two = np.cos(angle_two), np.sin(angle_two)
    first_hi, first_lo = split_table(np.concatenate([cos_one, -sin_one], 0))
    first = np.concatenate([first_hi, first_lo], 1)
    fwd_hi, fwd_lo = split_table(np.block([[cos_two, -sin_two], [sin_two, cos_two]]))
    inv_hi, inv_lo = split_table(np.block([[cos_two, sin_two], [-sin_two, cos_two]]))
    last_hi, last_lo = split_table(np.concatenate([cos_one.T, -sin_one.T], 1))
    last = np.concatenate([last_hi, last_lo], 0)
    pick = np.zeros((256, 256), np.float32)
    for dest in range(32):
        for row in range(4):
            part, at = row // 2, row % 2
            pick[128 * part + 4 * dest + at, 4 * dest + row] = 1.0
            pick[128 * part + 4 * dest + 2 + at, 128 + 4 * dest + row] = 1.0
    wide = np.stack([first, fwd_hi, fwd_lo, inv_hi, inv_lo, last, pick.astype(jnp.bfloat16)])
    eye = np.eye(n, dtype=np.float32).astype(jnp.bfloat16)
    mid = np.stack([np.cos(angle_mid), np.sin(angle_mid)]).astype(np.float32)
    return wide, eye, mid


def mm(a, b):
    return jnp.dot(a, b, preferred_element_type=F32)


def mm_t(a, b):
    return lax.dot_general(a, b, (((1,), (1,)), ((), ())), preferred_element_type=F32)


def split(x):
    high = x.astype(BF16)
    return high, (x - high.astype(F32)).astype(BF16)


def kernel(
    dims,
    vals_hbm,
    gate_hbm,
    grad_hbm,
    filt_hbm,
    skip_hbm,
    wide_hbm,
    mid_hbm,
    eye_hbm,
    gval_ref,
    ggate_ref,
    whole_ref,
    vals_ref,
    gate_ref,
    grad_ref,
    filt_ref,
    skip_ref,
    wide_ref,
    mid_ref,
    eye_ref,
    out_box,
    in_box,
    back_box,
    home_ref,
    rows,
    hspec,
    spec,
    own,
    cross,
    parts,
    total,
    load_sems,
    sems,
    arrived,
    returned,
    ready,
):
    n, seqs, nx, nz, ny, nc = dims
    ctx = n
    chans = 4
    me = lax.axis_index("ctx")
    my_seq = lax.axis_index("dp")

    loads = []
    for i, (src, dst) in enumerate(
        (
            (grad_hbm, grad_ref),
            (gate_hbm, gate_ref),
            (vals_hbm, vals_ref),
            (wide_hbm, wide_ref),
            (filt_hbm, filt_ref),
            (mid_hbm, mid_ref),
            (skip_hbm, skip_ref),
            (eye_hbm, eye_ref),
        )
    ):
        loads.append(pltpu.make_async_copy(src, dst, load_sems.at[i]))
        loads[-1].start()

    my_c = lax.rem(me, nc)
    my_y = lax.rem(me // nc, ny)
    my_z = lax.rem(me // (nc * ny), nz)
    my_x = me // (nc * ny * nz)
    x_part = [lax.rem(my_x + d, nx) * (nz * ny * nc) for d in range(nx)]
    z_part = [lax.rem(my_z + d, nz) * (ny * nc) for d in range(nz)]
    c_part = [lax.rem(my_c + d, nc) for d in range(nc)]
    x_far = sorted(range(nx), key=lambda d: -min(d, nx - d))
    lines = [x_part[d] + z + c for d in x_far for c in c_part[::-1] for z in z_part[::-1]]

    def each_peer(visit):
        def planes(step, carry):
            up = lax.rem(my_y + (ny // 2 - step), ny) * nc
            down = lax.rem(my_y + (ny // 2 + step), ny) * nc
            for line in lines:
                visit(line + up)
                visit(line + down)
            return carry

        across = lax.rem(my_y + ny // 2, ny) * nc
        for line in lines:
            visit(line + across)
        lax.fori_loop(1, ny // 2, planes, 0)
        for line in lines[:-1]:
            visit(line + my_y * nc)

    barrier = pltpu.get_barrier_semaphore()

    def greet(peer):
        pl.semaphore_signal(
            barrier, inc=1, device_id=(my_seq, peer), device_id_type=MESH
        )

    each_peer(greet)
    others = [lax.rem(my_seq + d, seqs) for d in range(seqs)]
    for d in range(1, seqs):

        @pl.when(my_seq + d < seqs)
        def _(d=d):
            pl.semaphore_signal(
                barrier, inc=1, device_id=(others[d], me), device_id_type=MESH
            )

    for load in loads[:4]:
        load.wait()
    first, fwd_hi, fwd_lo = wide_ref[0], wide_ref[1], wide_ref[2]
    inv_hi, inv_lo, last, pick = wide_ref[3], wide_ref[4], wide_ref[5], wide_ref[6]

    for g in range(chans):
        cols = slice(128 * g, 128 * (g + 1))
        gated = (grad_ref[:, cols].astype(F32) * gate_ref[:, cols].astype(F32)).astype(BF16)
        both = jnp.concatenate([vals_ref[:, cols], gated], 1)
        mail = mm_t(pick, both).astype(BF16)
        for part in range(2):
            out_box[part, 32 * g : 32 * (g + 1)] = mail[n * part : n * (part + 1)].reshape(32, 4, n)

    pl.semaphore_wait(barrier, ctx - 1 + my_seq)

    def exchange(src, dst, send_sem, recv_sem):
        def send(peer):
            pltpu.make_async_remote_copy(
                src_ref=src.at[peer],
                dst_ref=dst.at[me],
                send_sem=send_sem,
                recv_sem=recv_sem,
                device_id=(my_seq, peer),
                device_id_type=MESH,
            ).start()

        each_peer(send)
        pltpu.make_async_copy(src.at[me], dst.at[me], recv_sem).start()

    def drain(box, sem, count):
        part = box.at[pl.ds(0, count)]
        pltpu.make_async_copy(part, part, sem).wait()

    for part in range(2):
        exchange(out_box.at[part], in_box.at[part], sems.at[part], arrived.at[part])
    for d in range(1, seqs):

        @pl.when(my_seq + d >= seqs)
        def _(d=d):
            pl.semaphore_signal(
                ready, inc=1, device_id=(others[d], me), device_id_type=MESH
            )

    for load in loads[4:]:
        load.wait()
    cos_mid, sin_mid = mid_ref[0], mid_ref[1]

    def forward(blocks, exact):
        count = len(blocks)
        data = jnp.concatenate(blocks, 1)
        if exact:
            data = data.astype(BF16)
            part = mm(first, jnp.concatenate([data, data], 0))
        else:
            high, low = split(data)
            part = mm(first, jnp.concatenate([high, high], 0)) + mm(first[:, :n], low)
        turned = []
        for i in range(count):
            re = part[:n, n * i : n * (i + 1)]
            im = part[n:, n * i : n * (i + 1)]
            turned.append(
                jnp.concatenate([re * cos_mid + im * sin_mid, im * cos_mid - re * sin_mid], 1)
            )
        high, low = split(jnp.concatenate(turned, 0))
        return mm(high, fwd_hi) + (mm(low, fwd_hi) + mm(high, fwd_lo))

    def inverse(re, im):
        high, low = split(jnp.concatenate([re, im], 1))
        part = mm(high, inv_hi) + (mm(low, inv_hi) + mm(high, inv_lo))
        res, ims = [], []
        for i in range(part.shape[0] // n):
            re = part[n * i : n * (i + 1), :n]
            im = part[n * i : n * (i + 1), n:]
            res.append(re * cos_mid - im * sin_mid)
            ims.append(im * cos_mid + re * sin_mid)
        high, low = split(
            jnp.concatenate([jnp.concatenate(res, 1), jnp.concatenate(ims, 1)], 0)
        )
        both = mm(last, high)
        return both[:n] + (both[n:] + mm(last[:n], low))

    scale = float(n) ** -1
    unit = float(n) ** -2
    h = forward([filt_ref[pl.ds(c, n, stride=chans), :] for c in range(chans)], False)
    for c in range(chans):
        band = slice(n * c, n * (c + 1))
        hspec[band, :n] = (h[band, :n] * scale + skip_ref[c]) * unit
        hspec[band, n:] = h[band, n:] * (scale * unit)

    early = my_seq < seqs // 2
    far_first = sorted(range(1, seqs), key=lambda d: -min(d, seqs - d))
    pair = 2 * n

    def send_parts(channels):
        for d in far_first:

            @pl.when(others[d] // 2 == channels)
            def _(d=d):
                pltpu.make_async_remote_copy(
                    src_ref=cross.at[others[d]],
                    dst_ref=parts.at[d - 1],
                    send_sem=sems.at[4],
                    recv_sem=sems.at[5],
                    device_id=(others[d], me),
                    device_id_type=MESH,
                ).start()

    def wait_ready():
        @pl.when(my_seq < seqs - 1)
        def _():
            pl.semaphore_wait(ready, seqs - 1 - my_seq)

    def results_of(part):
        v_re, v_im = spec[part, :pair, :n], spec[part, :pair, n:]
        d_re, d_im = spec[part, pair:, :n], spec[part, pair:, n:]
        band = slice(pair * part, pair * (part + 1))
        h_re, h_im = hspec[band, :n], hspec[band, n:]
        conv = inverse(h_re * v_re - h_im * v_im, h_re * v_im + h_im * v_re)
        gval = inverse(h_re * d_re + h_im * d_im, h_re * d_im - h_im * d_re)
        for c in range(2):
            rows[pl.ds(c, n, stride=4), :] = conv[:, n * c : n * (c + 1)]
            rows[pl.ds(2 + c, n, stride=4), :] = gval[:, n * c : n * (c + 1)]
        back_box[part] = rows[...].reshape(n, 4, n).astype(BF16)

    def send_back(part):
        exchange(back_box.at[part], home_ref.at[part], sems.at[2 + part], returned.at[part])

    for part in range(2):
        pltpu.make_async_copy(in_box.at[part], in_box.at[part], arrived.at[part]).wait()
        rows[...] = in_box[part].astype(F32).reshape(4 * n, n)
        spec[part] = forward([rows[pl.ds(c, n, stride=4), :] for c in range(4)], True)
        v_re, v_im = spec[part, :pair, :n], spec[part, :pair, n:]
        d_re, d_im = spec[part, pair:, :n], spec[part, pair:, n:]
        lag = inverse(d_re * v_re + d_im * v_im, d_im * v_re - d_re * v_im)
        lag = lag * (unit * (seqs**-0.5) * scale)
        for c in range(2):
            own[2 * part + c] = lag[:, n * c : n * (c + 1)]
            cross[2 * part + c] = lag[:, n * c : n * (c + 1)].astype(BF16)
        if part == 0:

            @pl.when(jnp.logical_not(early))
            def _():
                wait_ready()
                send_parts(0)

        else:

            @pl.when(early)
            def _():
                wait_ready()
                send_parts(0)

            send_parts(1)

    for part in range(2):
        results_of(part)

    @pl.when(early)
    def _():
        for part in range(2):
            send_back(part)

    drain(parts, sems.at[5], seqs - 1)
    summed = own[my_seq]
    for d in range(seqs - 1):
        summed = summed + parts[d].astype(F32)
    total[0] = summed.astype(BF16)
    for d in far_first:
        pltpu.make_async_remote_copy(
            src_ref=total.at[0],
            dst_ref=whole_ref.at[my_seq],
            send_sem=sems.at[6],
            recv_sem=sems.at[7],
            device_id=(others[d], me),
            device_id_type=MESH,
        ).start()
    pltpu.make_async_copy(total.at[0], whole_ref.at[my_seq], sems.at[7]).start()

    @pl.when(jnp.logical_not(early))
    def _():
        for part in range(2):
            send_back(part)

    for part in range(2):
        drain(out_box.at[part], sems.at[part], ctx - 1)
        drain(back_box.at[part], sems.at[2 + part], ctx - 1)
    drain(cross, sems.at[4], seqs - 1)
    drain(cross, sems.at[6], seqs - 1)
    for part in range(2):
        drain(home_ref.at[part], returned.at[part], ctx)
    for g in range(chans):
        cols = slice(128 * g, 128 * (g + 1))
        group = jnp.concatenate(
            [home_ref[part, 32 * g : 32 * (g + 1)].reshape(128, n) for part in range(2)], 0
        )
        both = mm(mm_t(eye_ref[...], group).astype(BF16), pick)
        gval_ref[:, cols] = both[:, n:].astype(BF16)
        ggate_ref[:, cols] = (grad_ref[:, cols].astype(F32) * both[:, :n]).astype(BF16)
    drain(whole_ref, sems.at[7], seqs)


def finish(gval_in, ggate_in, whole_ref, gval_hbm, ggate_hbm, gfilt_hbm, gfilt_ref, sems):
    seqs, n = whole_ref.shape[:2]
    copies = [
        pltpu.make_async_copy(gval_in, gval_hbm, sems.at[0]),
        pltpu.make_async_copy(ggate_in, ggate_hbm, sems.at[1]),
        pltpu.make_async_copy(gfilt_ref, gfilt_hbm, sems.at[2]),
    ]
    copies[0].start()
    copies[1].start()
    for c in range(seqs):
        gfilt_ref[pl.ds(c, n, stride=seqs), :] = whole_ref[c].astype(F32)
    copies[2].start()
    for copy in copies:
        copy.wait()


def per_device(sizes, values, gates, grad_out, filters, skip):
    seqs, ctx = sizes
    length = filters.shape[1]
    n = values.shape[1]
    chans = filters.shape[0]
    wide, eye, mid = (jnp.asarray(t) for t in make_tables(n))
    filt = filters.reshape(chans, n, n).transpose(1, 0, 2).reshape(n * chans, n)
    vmem = pl.BlockSpec(memory_space=pltpu.VMEM)
    anywhere = pl.BlockSpec(memory_space=pl.ANY)
    in_hbm = pl.BlockSpec(memory_space=pltpu.HBM)
    gval, ggate, whole = pl.pallas_call(
        functools.partial(kernel, (n, seqs, 4, 2, 8, 2)),
        name="hyena_bwd",
        out_shape=(
            pltpu.VMEM((n, chans * n), BF16),
            pltpu.VMEM((n, chans * n), BF16),
            pltpu.VMEM((seqs, n, n), BF16),
        ),
        in_specs=[in_hbm] * 8,
        out_specs=(vmem, vmem, anywhere),
        scratch_shapes=[
            pltpu.VMEM((n, chans * n), BF16),
            pltpu.VMEM((n, chans * n), BF16),
            pltpu.VMEM((n, chans * n), BF16),
            pltpu.VMEM((n * chans, n), F32),
            pltpu.SMEM((chans,), F32),
            pltpu.VMEM(wide.shape, BF16),
            pltpu.VMEM(mid.shape, F32),
            pltpu.VMEM(eye.shape, BF16),
            pltpu.VMEM((2, n, 4, n), BF16),
            pltpu.VMEM((2, n, 4, n), BF16),
            pltpu.VMEM((2, n, 4, n), BF16),
            pltpu.VMEM((2, n, 4, n), BF16),
            pltpu.VMEM((4 * n, n), F32),
            pltpu.VMEM((chans * n, 2 * n), F32),
            pltpu.VMEM((2, chans * n, 2 * n), F32),
            pltpu.VMEM((chans, n, n), F32),
            pltpu.VMEM((chans, n, n), BF16),
            pltpu.VMEM((seqs - 1, n, n), BF16),
            pltpu.VMEM((1, n, n), BF16),
            pltpu.SemaphoreType.DMA((8,)),
            pltpu.SemaphoreType.DMA((8,)),
            pltpu.SemaphoreType.DMA((2,)),
            pltpu.SemaphoreType.DMA((2,)),
            pltpu.SemaphoreType.REGULAR,
        ],
        compiler_params=pltpu.CompilerParams(
            collective_id=0, has_side_effects=True, vmem_limit_bytes=60 * 1024 * 1024
        ),
    )(values[0], gates[0], grad_out[0], filt, skip, wide, mid, eye)
    gval, ggate, gfilt = pl.pallas_call(
        finish,
        name="hyena_out",
        out_shape=(
            jax.ShapeDtypeStruct(values.shape[1:], BF16),
            jax.ShapeDtypeStruct(values.shape[1:], BF16),
            jax.ShapeDtypeStruct((n * chans, n), F32),
        ),
        in_specs=[vmem] * 3,
        out_specs=(in_hbm,) * 3,
        scratch_shapes=[
            pltpu.VMEM((n * chans, n), F32),
            pltpu.SemaphoreType.DMA((3,)),
        ],
        compiler_params=pltpu.CompilerParams(vmem_limit_bytes=8 << 20),
    )(gval, ggate, whole)
    gfilt = gfilt.reshape(n, chans, n).transpose(1, 0, 2).reshape(chans, length)
    return gval[None], ggate[None], gfilt


def solution(mesh):
    in_specs = (
        P("dp", "ctx", None),
        P("dp", "ctx", None),
        P("dp", "ctx", None),
        P("ctx", None),
        P("ctx"),
    )
    out_specs = (P("dp", "ctx", None), P("dp", "ctx", None), P("ctx", None))
    return jax.shard_map(
        functools.partial(per_device, (mesh.shape["dp"], mesh.shape["ctx"])),
        mesh=mesh,
        in_specs=in_specs,
        out_specs=out_specs,
        check_vma=False,
    )
```
